512 devices in a mesh: gx: 64 (over z, x), gy: 8 (over y, core).
Axes of the slice: x: 4, y: 4, z: 16, core: 2. Of those that a mesh axis runs over, the one named last changes fastest.
Arguments:
- velocity: float32 [3, 512, 384, 256], P(None, 'gx', 'gy'), may hold values from -6 to 6
- pressure: float32 [512, 384, 256], P('gx', 'gy'), may hold values from -6 to 6
- viscosity: float32 [512, 384, 256], P('gx', 'gy'), may hold values from 0.12 to 0.6
- wind_profile: float32 [256], replicated, may hold values from 0.5 to 1.5
- panel_area: float32 [16384], P('gy'), may hold values from 0.5 to 2
- slot_cell: int32 [8, 4096], P('gy', 'gx'), may hold values from 0 to 98303
- slot_panel: int32 [8, 4096], P('gy'), may hold values from -1 to 2047, as said below
- panel_shapes: bfloat16 [16384, 2048], P('gy', 'gx'), may hold values from -0.046875 to 0.046875
- node_shapes: bfloat16 [1024, 2048], P(None, 'gx'), may hold values from -0.125 to 0.125
- damper_node: int32 [512], P('gy'), may hold values from 0 to 1022
- damper_viscous: float32 [512], P('gy'), may hold values from 0.2 to 2
- damper_hysteretic: float32 [512], P('gy'), may hold values from 0.2 to 2
- frequency: float32 [2048], P('gx'), may hold values from 0.2 to 1.8
- damping_ratio: float32 [2048], P('gx'), may hold values from 0.05 to 0.5
- modal_state: float32 [2, 2048], P(None, 'gx'), may hold values from -6 to 6
- damper_state: float32 [512], P('gy'), may hold values from -1 to 1
Outputs:
- velocity_next: float32 [3, 512, 384, 256], P(None, 'gx', 'gy')
- pressure_next: float32 [512, 384, 256], P('gx', 'gy')
- modal_next: float32 [2, 2048], P(None, 'gx')
- damper_next: float32 [512], P('gy')
The draws below stay inside these ranges and needn't reach their ends.
Inputs may be any that keep to these rules, and one draw needn't show every extreme that they name: `slot_panel`: in every row each panel number 0 to 2047 stands in exactly one slot; every other slot holds -1.
All inputs are finite; a program needn't handle non-finite values.
Results may differ from the reference program's by a relative error of at most 0.0013.
Values may be sent and summed in bfloat16 or wider, within the bound.
A program may use at most 64 MiB of HBM per device.

```python
import math
import jax
import jax.numpy as jnp
from jax import lax

CX = 8
CY = 48
NZ = 256
MODES = 2048
PAN_COL = 2048
NODES = 1024
SLOTS = 64
NX = 512
NY = 384
PANELS = 16384
DAMPERS = 512
N_GX = 64
N_GY = 8


def draw_slot_panel(key, part):
    piece_total = NY // CY
    slot_total = NX // CX * SLOTS
    piece_keys = jax.random.split(key, piece_total)
    orders = jax.vmap(lambda single: jax.random.permutation(single, slot_total))(piece_keys).astype(jnp.int32)
    return jnp.where(orders < PAN_COL, orders, -1).astype(jnp.int32)


def set_ends(values, key, smallest, largest):
    longest = values.shape.index(max(values.shape))
    spots = []
    for shift in (0, 1):
        where = [jax.random.randint(jax.random.fold_in(key, axis), (), 0, length) for axis, length in enumerate(values.shape)]
        where[longest] = (where[longest] + shift) % values.shape[longest]
        spots.append(tuple(where))
    return values.at[spots[0]].set(smallest).at[spots[1]].set(largest)


def block_scale(rng, shape, shards, smallest, largest):
    factor_of = 1.0
    for position, parts in shards:
        steps = jax.random.uniform(jax.random.fold_in(jax.random.fold_in(rng, 6), position), (parts,), jnp.float32, smallest / len(shards), largest / len(shards))
        factor_of = factor_of * jnp.repeat(jnp.exp(steps), shape[position] // parts).reshape((-1,) + (1,) * (len(shape) - 1 - position))
    return factor_of


def noise(own_key, dims, deviation, most, cuts=(), kind=jnp.bfloat16):
    loudness = block_scale(own_key, dims, cuts, -0.22, 0.18) if cuts else 1.0
    drawn = jax.random.normal(own_key, dims, jnp.float32) * deviation * loudness
    return jnp.minimum(jnp.maximum(drawn, -most), most).astype(kind)


def setup_inputs(seed: int = 0) -> dict:
    key_list = jax.random.split(jax.random.key(seed), 17)
    velocity = noise(key_list[0], (3, NX, NY, NZ), 1.0, 6.0, ((1, 64), (2, 8)), jnp.float32)
    pressure = noise(key_list[1], (NX, NY, NZ), 1.0, 6.0, ((0, 64), (1, 8)), jnp.float32)
    viscosity = jnp.clip(jnp.exp(math.log(0.6) - 1.609438 * jax.random.uniform(key_list[2], (NX, NY, NZ), jnp.float32) ** block_scale(key_list[2], (NX, NY, NZ), ((0, 64), (1, 8)), -0.2, 0.2)), 0.12, 0.6)
    wind_profile = jnp.clip(jax.random.uniform(key_list[3], (NZ,), jnp.float32, 0.5, 1.5), 0.5, 1.5)
    panel_area = jnp.clip(jnp.exp(math.log(2.0) - 1.3862944 * jax.random.uniform(key_list[4], (PANELS,), jnp.float32) ** block_scale(key_list[4], (PANELS,), ((0, 8),), -0.2, 0.2)), 0.5, 2.0)
    slot_cell = set_ends(jax.random.randint(key_list[5], (N_GY, N_GX * SLOTS), 0, CX * CY * NZ), jax.random.fold_in(key_list[5], 1), 0, (CX * CY * NZ) - 1).astype(jnp.int32)
    slot_panel = draw_slot_panel(jax.random.fold_in(key_list[16], 71), 0)
    panel_shapes = noise(key_list[7], (PANELS, MODES), PANELS ** -0.5, 0.046875, ((0, 8), (1, 64)))
    node_shapes = noise(key_list[8], (NODES, MODES), MODES ** -0.5, 0.125, ((1, 64),))
    damper_node = set_ends(jax.random.randint(key_list[9], (DAMPERS,), 0, NODES - 1), jax.random.fold_in(key_list[9], 1), 0, (NODES - 1) - 1).astype(jnp.int32)
    damper_viscous = jnp.clip(jnp.exp(math.log(2.0) - 2.3025851 * jax.random.uniform(key_list[10], (DAMPERS,), jnp.float32) ** block_scale(key_list[10], (DAMPERS,), ((0, 8),), -0.2, 0.2)), 0.2, 2.0)
    damper_hysteretic = jnp.clip(jnp.exp(math.log(2.0) - 2.3025851 * jax.random.uniform(key_list[11], (DAMPERS,), jnp.float32) ** block_scale(key_list[11], (DAMPERS,), ((0, 8),), -0.2, 0.2)), 0.2, 2.0)
    frequency = jnp.clip(jnp.exp(math.log(1.8) - 2.1972245 * jax.random.uniform(key_list[12], (MODES,), jnp.float32) ** block_scale(key_list[12], (MODES,), ((0, 64),), -0.2, 0.2)), 0.2, 1.8)
    damping_ratio = jnp.clip(jnp.exp(math.log(0.5) - 2.3025851 * jax.random.uniform(key_list[13], (MODES,), jnp.float32) ** block_scale(key_list[13], (MODES,), ((0, 64),), -0.2, 0.2)), 0.05, 0.5)
    modal_state = noise(key_list[14], (2, MODES), 1.0, 6.0, ((1, 64),), jnp.float32)
    damper_state = jnp.clip(jax.random.uniform(key_list[15], (DAMPERS,), jnp.float32, -1.0, 1.0) * block_scale(key_list[15], (DAMPERS,), ((0, 8),), -0.4, 0.0), -1.0, 1.0)
    return {"velocity": velocity, "pressure": pressure, "viscosity": viscosity, "wind_profile": wind_profile, "panel_area": panel_area, "slot_cell": slot_cell, "slot_panel": slot_panel, "panel_shapes": panel_shapes, "node_shapes": node_shapes, "damper_node": damper_node, "damper_viscous": damper_viscous, "damper_hysteretic": damper_hysteretic, "frequency": frequency, "damping_ratio": damping_ratio, "modal_state": modal_state, "damper_state": damper_state}


time_step = 0.1
sound_squared = 1.0
modal_step = 0.5
hysteresis_gain = 1.0
shape_beta = 0.5
shape_gamma = 0.5
spring_rate = 0.5


def advance(padded, local_viscosity, wind_profile):
    centre_cells = padded[:, 1:-1, 1:-1, 1:-1]
    ahead_cells = padded[:, 2:, 1:-1, 1:-1]
    behind_cells = padded[:, :-2, 1:-1, 1:-1]
    right_cells = padded[:, 1:-1, 2:, 1:-1]
    left_cells = padded[:, 1:-1, :-2, 1:-1]
    above_cells = padded[:, 1:-1, 1:-1, 2:]
    below_cells = padded[:, 1:-1, 1:-1, :-2]
    slope_stream = 0.5 * (ahead_cells - behind_cells)
    slope_span = 0.5 * (right_cells - left_cells)
    slope_vertical = 0.5 * (above_cells - below_cells)
    laplacian = ahead_cells + behind_cells + right_cells + left_cells + above_cells + below_cells - 6.0 * centre_cells
    pressure_slope = jnp.stack([slope_stream[3], slope_span[3], slope_vertical[3]])
    velocity_new = centre_cells[:3] + time_step * (-wind_profile * slope_stream[:3] + local_viscosity * laplacian[:3] - pressure_slope)
    pressure_new = centre_cells[3] - time_step * sound_squared * (slope_stream[0] + slope_span[1] + slope_vertical[2])
    return jnp.concatenate([velocity_new, pressure_new[None]], axis=0)


def reference(velocity, pressure, viscosity, wind_profile, panel_area, slot_cell, slot_panel, panel_shapes, node_shapes, damper_node, damper_viscous, damper_hysteretic, frequency, damping_ratio, modal_state, damper_state):
    fields = jnp.concatenate([velocity, pressure[None]], axis=0)
    for substep in range(2):
        padded = jnp.pad(fields, ((0, 0), (1, 1), (1, 1), (1, 1)))

        def slab_update(slab_number, padded=padded):
            start = slab_number * CX
            piece = lax.dynamic_slice_in_dim(padded, start, CX + 2, 1)
            local_viscosity = lax.dynamic_slice_in_dim(viscosity, start, CX, 0)
            return advance(piece, local_viscosity, wind_profile)

        updated = lax.map(slab_update, jnp.arange(N_GX, dtype=jnp.int32))
        fields = jnp.moveaxis(updated, 0, 1).reshape(4, NX, NY, NZ)
    velocity_next = fields[:3]
    pressure_next = fields[3]

    pressure_blocks = pressure_next.reshape(N_GX, CX, N_GY, CY, NZ).transpose(2, 0, 1, 3, 4).reshape(N_GY, N_GX, CX * CY * NZ)
    cell_table = slot_cell.reshape(N_GY, N_GX, SLOTS)
    sampled = jnp.take_along_axis(pressure_blocks, cell_table, axis=2).reshape(N_GY, N_GX * SLOTS)
    area_table = panel_area.reshape(N_GY, PAN_COL)
    safe_ids = jnp.where(slot_panel < 0, 0, slot_panel).astype(jnp.int32)
    slot_load = (jnp.take_along_axis(area_table, safe_ids, axis=1) * sampled).astype(jnp.bfloat16)
    target = jnp.where(slot_panel < 0, PAN_COL, slot_panel).astype(jnp.int32)

    def place(row_target, row_loads):
        return jnp.zeros((PAN_COL + 1,), jnp.bfloat16).at[row_target].set(row_loads)[:PAN_COL]

    panel_load = jax.vmap(place)(target, slot_load).reshape(PANELS)
    panel_modal = jnp.dot(panel_load, panel_shapes, preferred_element_type=jnp.float32)

    drift = node_shapes[damper_node + 1].astype(jnp.float32) - node_shapes[damper_node].astype(jnp.float32)
    displacement = modal_state[0]
    modal_velocity = modal_state[1]
    hysteresis = damper_state
    for modal_turn in range(2):
        stretch = jnp.dot(drift, displacement, precision=lax.Precision.HIGHEST)
        stretch_rate = jnp.dot(drift, modal_velocity, precision=lax.Precision.HIGHEST)
        hysteresis = hysteresis + modal_step * (hysteresis_gain * stretch_rate - shape_beta * jnp.abs(stretch_rate) * hysteresis - shape_gamma * stretch_rate * jnp.abs(hysteresis))
        damper_force = -(damper_viscous * stretch_rate + spring_rate * stretch + damper_hysteretic * hysteresis)
        modal_load = panel_modal + jnp.dot(damper_force, drift, precision=lax.Precision.HIGHEST)
        acceleration = modal_load - 2.0 * damping_ratio * frequency * modal_velocity - frequency * frequency * displacement
        modal_velocity = modal_velocity + modal_step * acceleration
        displacement = displacement + modal_step * modal_velocity
    return velocity_next, pressure_next, jnp.stack([displacement, modal_velocity]), hysteresis
```

```python
import jax
import jax.numpy as jnp
from jax import lax
from jax.experimental import pallas as pl
from jax.experimental.pallas import tpu as pltpu
from jax.sharding import PartitionSpec as P

time_step = 0.1
sound_squared = 1.0
modal_step = 0.5
hysteresis_gain = 1.0
shape_beta = 0.5
shape_gamma = 0.5
spring_rate = 0.5

CX, CY, NZ = 8, 48, 256
NGX, NGY = 64, 8
MB = 32
DB = 64
SL = 64
Y0 = 8
YT = CY // 8


def row_of(column, lane_shift=0, lanes=128):
    n = column.shape[0]
    sub = lax.broadcasted_iota(jnp.int32, (n, lanes), 0)
    lane = lax.broadcasted_iota(jnp.int32, (n, lanes), 1)
    return jnp.sum(jnp.where(lane == sub + lane_shift, column, 0.0), axis=0, keepdims=True)


def column_of(row, n, lane_shift=0):
    lanes = row.shape[1]
    sub = lax.broadcasted_iota(jnp.int32, (n, lanes), 0)
    lane = lax.broadcasted_iota(jnp.int32, (n, lanes), 1)
    zero = jnp.zeros((), row.dtype)
    return jnp.sum(jnp.where(lane == sub + lane_shift, row, zero), axis=1, keepdims=True)


def kernel(
    vel_h, pre_h, vis_h, wind, area, cell_s, cell_v, panels, shapes_t, nodes_t,
    dnode, dvisc, dhyst, freq, ratio, modal, dstate,
    vel_o, pre_o, modal_o, damp_o,
    f0, f1, vis, xs, xr, ys, yr, samp, onehot, lhs, g0, h1, g2, h3,
    in_sem, xss, xrs, yss, yrs, s_sem, r_sem,
):
    gx = lax.axis_index("gx")
    gy = lax.axis_index("gy")
    f32, bf16 = jnp.float32, jnp.bfloat16

    def gx_peer(k):
        return {"gx": lax.rem(gx + k, NGX)}

    def gy_peer(k):
        return {"gy": lax.rem(gy + k, NGY)}

    barrier = pltpu.get_barrier_semaphore()

    def greet_gx(k, carry):
        pl.semaphore_signal(barrier, 1, device_id=gx_peer(k))
        return carry

    def greet_gy(k, carry):
        pl.semaphore_signal(barrier, 1, device_id=gy_peer(k))
        return carry

    lax.fori_loop(1, NGX, greet_gx, 0)
    lax.fori_loop(1, NGY, greet_gy, 0)
    cv = pltpu.make_async_copy(vel_h, f0.at[0:3, 1 : 1 + CX, Y0 : Y0 + CY, :], in_sem.at[0])
    cp = pltpu.make_async_copy(pre_h, f0.at[3, 1 : 1 + CX, Y0 : Y0 + CY, :], in_sem.at[1])
    cn = pltpu.make_async_copy(vis_h, vis, in_sem.at[2])
    cv.start()
    cp.start()
    cn.start()
    cv.wait()
    cp.wait()

    y_order = (1, 0, 2, 3)

    def pack_x(f, p, comps):
        for k in comps:
            xs[p, 0, k] = f[k, CX, Y0 : Y0 + CY, :].astype(bf16)
            xs[p, 1, k] = f[k, 1, Y0 : Y0 + CY, :].astype(bf16)

    def pack_y(f, p, slots):
        for q in slots:
            k = y_order[q]
            for x in range(CX):
                ys[p, 0, q, x : x + 1, :] = f[k, x + 1, Y0 + CY - 1 : Y0 + CY, :]
                ys[p, 1, q, x : x + 1, :] = f[k, x + 1, Y0 : Y0 + 1, :]

    def x_copy(p, part, d, lo, hi):
        i = 2 * part + d
        return pltpu.make_async_remote_copy(
            xs.at[p, d, lo:hi], xr.at[p, d, lo:hi], xss.at[p, i], xrs.at[p, i],
            device_id=gx_peer(1 if d == 0 else NGX - 1),
        )

    def y_copy(p, part, d, lo, hi):
        i = 2 * part + d
        return pltpu.make_async_remote_copy(
            ys.at[p, d, lo:hi], yr.at[p, d, lo:hi], yss.at[p, i], yrs.at[p, i],
            device_id=gy_peer(1 if d == 0 else NGY - 1),
        )

    def unpack_x(f, p, comps):
        for k in comps:
            f[k, 0, Y0 : Y0 + CY, :] = jnp.where(gx == 0, 0.0, xr[p, 0, k].astype(f32))
            f[k, CX + 1, Y0 : Y0 + CY, :] = jnp.where(gx == NGX - 1, 0.0, xr[p, 1, k].astype(f32))

    def unpack_y(f, p, slots):
        for q in slots:
            k = y_order[q]
            for x in range(CX):
                f[k, x + 1, Y0 - 1 : Y0, :] = jnp.where(gy == 0, 0.0, yr[p, 0, q, x : x + 1, :])
                f[k, x + 1, Y0 + CY : Y0 + CY + 1, :] = jnp.where(
                    gy == NGY - 1, 0.0, yr[p, 1, q, x : x + 1, :]
                )

    pack_x(f0, 0, range(4))
    pack_y(f0, 0, range(4))
    pl.semaphore_wait(barrier, NGX - 1 + NGY - 1)
    hx1 = [x_copy(0, 0, d, 0, 4) for d in range(2)]
    hy1 = [y_copy(0, 0, d, 0, 4) for d in range(2)]
    for c in hy1 + hx1:
        c.start()

    dn = dnode[...]
    dn2 = jnp.concatenate([dn, dn], axis=1)
    node_no = lax.broadcasted_iota(jnp.int32, (nodes_t.shape[1], 2 * DB), 0)
    pick = jnp.where(node_no == dn2 + 1, 1.0, jnp.where(node_no == dn2, -1.0, 0.0)).astype(bf16)
    drift = jnp.dot(nodes_t[...], pick, preferred_element_type=f32)
    q0 = column_of(modal[0:1, :], MB)
    v0 = column_of(modal[1:2, :], MB)
    omega = column_of(freq[...], MB)
    zeta = column_of(ratio[...], MB)
    first_half = lax.broadcasted_iota(jnp.int32, (MB, 2 * DB), 1) < DB

    def stretch_row(q, v):
        return jnp.sum(drift * jnp.where(first_half, q, v), axis=0, keepdims=True)

    g0[gx, 1:2, :] = stretch_row(q0, v0)

    def table(i, carry):
        low = panels[pl.ds(i, 1), :] & 127
        sub = lax.broadcasted_iota(jnp.int32, (128, 128), 0)
        onehot[:, pl.ds(pl.multiple_of(i * 128, 128), 128)] = (sub == low).astype(f32).astype(bf16)
        return carry

    lax.fori_loop(0, panels.shape[0], table, 0)
    parity = lax.rem(gx, 2)
    own_ids = column_of(panels[pl.ds(gx // 2, 1), :], SL, SL * parity)
    panel_no = lax.broadcasted_iota(jnp.int32, (SL, area.shape[1]), 1)
    own_area = jnp.sum(jnp.where(panel_no == own_ids, area[...], 0.0), axis=1, keepdims=True)
    own_z = column_of(cell_v[...], SL) & (NZ - 1)
    z_mask = (lax.broadcasted_iota(jnp.int32, (SL, NZ), 1) == own_z)

    lane8 = lax.broadcasted_iota(jnp.int32, (8, NZ), 1)

    def above(v):
        return jnp.where(lane8 == NZ - 1, 0.0, pltpu.roll(v, NZ - 1, 1))

    def below(v):
        return jnp.where(lane8 == 0, 0.0, pltpu.roll(v, 1, 1))

    w_row = jnp.broadcast_to((-0.5 * time_step) * wind[...], (8, NZ))
    half = 0.5 * time_step

    def velocity_tile(f, x, t):
        rows = pl.ds(Y0 + 8 * t, 8)
        rows_m = pl.ds(Y0 + 8 * t - 1, 8)
        rows_p = pl.ds(Y0 + 8 * t + 1, 8)
        nu = time_step * vis[x - 1, 8 * t : 8 * t + 8, :]
        pc = f[3, x, rows, :]
        slope = (
            f[3, x + 1, rows, :] - f[3, x - 1, rows, :],
            f[3, x, rows_p, :] - f[3, x, rows_m, :],
            above(pc) - below(pc),
        )
        out = []
        for k in range(3):
            c = f[k, x, rows, :]
            a, b = f[k, x + 1, rows, :], f[k, x - 1, rows, :]
            r, l = f[k, x, rows_p, :], f[k, x, rows_m, :]
            u, d = above(c), below(c)
            lap = ((a + b) + (r + l)) + ((u + d) - 6.0 * c)
            out.append(c + (w_row * (a - b) + nu * lap - half * slope[k]))
        return out

    def pressure_tile(f, x, t):
        rows = pl.ds(Y0 + 8 * t, 8)
        rows_m = pl.ds(Y0 + 8 * t - 1, 8)
        rows_p = pl.ds(Y0 + 8 * t + 1, 8)
        w = f[2, x, rows, :]
        div = (f[0, x + 1, rows, :] - f[0, x - 1, rows, :]) + (
            (f[1, x, rows_p, :] - f[1, x, rows_m, :]) + (above(w) - below(w))
        )
        return f[3, x, rows, :] - (half * sound_squared) * div

    def first_layer(x, carry):
        for t in range(YT):
            rows = slice(Y0 + 8 * t, Y0 + 8 * t + 8)
            new = velocity_tile(f0, x, t)
            for k in range(3):
                f1[k, x, rows, :] = new[k]
            f1[3, x, rows, :] = pressure_tile(f0, x, t)
        return carry

    cn.wait()
    for c in hy1:
        c.wait_recv()
    unpack_y(f0, 0, range(4))
    lax.fori_loop(2, CX, first_layer, 0)
    for c in hx1:
        c.wait_recv()
    unpack_x(f0, 0, range(4))
    first_layer(1, 0)
    first_layer(CX, 0)

    pack_x(f1, 1, (0,))
    pack_y(f1, 1, (0,))
    hx2 = [x_copy(1, 0, d, 0, 1) for d in range(2)]
    hy2 = [y_copy(1, 0, d, 0, 1) for d in range(2)]
    for c in hx2 + hy2:
        c.start()
    pack_x(f1, 1, (1, 2, 3))
    pack_y(f1, 1, (1, 2, 3))
    hx3 = [x_copy(1, 1, d, 1, 4) for d in range(2)]
    hy3 = [y_copy(1, 1, d, 1, 4) for d in range(2)]
    for c in hx3 + hy3:
        c.start()
    for c in hx2 + hy2:
        c.wait_recv()
    unpack_x(f1, 1, (0,))
    unpack_y(f1, 1, (0,))

    def second_pressure(x, carry):
        for t in range(YT):
            pre_o[x - 1, 8 * t : 8 * t + 8, :] = pressure_tile(f1, x, t)
        return carry

    lax.fori_loop(1, CX + 1, second_pressure, 0)

    for s in range(SL):
        line = cell_s[0, s] >> 8
        plane = line // CY
        samp[s : s + 1, :] = pre_o[plane, pl.ds(line - plane * CY, 1), :]
    sampled = jnp.sum(jnp.where(z_mask, samp[...], 0.0), axis=1, keepdims=True)
    load = (own_area * sampled).astype(bf16).astype(f32)
    g0[gx, 0:1, :] = row_of(load, SL * parity)

    def all_gx(buf, sem_no):
        def send(k, carry):
            pltpu.make_async_remote_copy(
                buf.at[gx], buf.at[gx], s_sem.at[sem_no], r_sem.at[sem_no], device_id=gx_peer(k)
            ).start()
            return carry

        lax.fori_loop(1, NGX, send, 0)
        most = buf.at[pl.ds(0, NGX - 1)]
        return pltpu.make_async_remote_copy(
            most, most, s_sem.at[sem_no], r_sem.at[sem_no], device_id=gx_peer(1)
        )

    def all_gy(buf, sem_no):
        def send(k, carry):
            pltpu.make_async_remote_copy(
                buf.at[gy], buf.at[gy], s_sem.at[sem_no], r_sem.at[sem_no], device_id=gy_peer(k)
            ).start()
            return carry

        lax.fori_loop(1, NGY, send, 0)
        most = buf.at[pl.ds(0, NGY - 1)]
        return pltpu.make_async_remote_copy(
            most, most, s_sem.at[sem_no], r_sem.at[sem_no], device_id=gy_peer(1)
        )

    stage0 = all_gx(g0, 0)
    for c in hx3 + hy3:
        c.wait_recv()
    unpack_x(f1, 1, (1, 2, 3))
    unpack_y(f1, 1, (1, 2, 3))

    def second_velocity(x, carry):
        for t in range(YT):
            new = velocity_tile(f1, x, t)
            for k in range(3):
                vel_o[k, x - 1, 8 * t : 8 * t + 8, :] = new[k]
        return carry

    lax.fori_loop(1, CX + 1, second_velocity, 0)
    for c in hx1 + hy1 + hx2 + hy2 + hx3 + hy3:
        c.wait_send()

    stage0.wait_recv()
    sub16 = lax.broadcasted_iota(jnp.int32, (16, 128), 0)
    for i in range(NGX // 2):
        pair = g0[2 * i, 0:1, :] + g0[2 * i + 1, 0:1, :]
        high = panels[i : i + 1, :] >> 7
        lhs[:, i * 128 : (i + 1) * 128] = jnp.where(sub16 == high, pair, 0.0).astype(bf16)
    placed = lax.dot_general(
        lhs[...], onehot[...], (((1,), (1,)), ((), ())), preferred_element_type=f32
    )
    part = jnp.zeros((MB, 128), f32)
    for a in range(16):
        part = part + shapes_t[:, a * 128 : (a + 1) * 128].astype(f32) * placed[a : a + 1, :]
    panel_part = jnp.sum(part, axis=1, keepdims=True)

    def response(total, hysteresis):
        stretch = total[:, 0:DB]
        rate = total[:, DB : 2 * DB]
        hysteresis = hysteresis + modal_step * (
            hysteresis_gain * rate
            - shape_beta * jnp.abs(rate) * hysteresis
            - shape_gamma * rate * jnp.abs(hysteresis)
        )
        force = -(dvisc[...] * rate + spring_rate * stretch + dhyst[...] * hysteresis)
        return hysteresis, jnp.sum(drift[:, 0:DB] * force, axis=1, keepdims=True)

    hysteresis, damper_part = response(jnp.sum(g0[:, 1:2, :], axis=0), dstate[...])
    h1[gy] = row_of(panel_part) + row_of(damper_part, MB)
    stage1 = all_gy(h1, 1)
    stage0.wait_send()
    stage1.wait_recv()
    total1 = jnp.sum(h1[...], axis=0)
    panel_modal = column_of(total1, MB)

    def advance_modes(q, v, damper_load):
        acceleration = (
            panel_modal + damper_load - 2.0 * zeta * omega * v - omega * omega * q
        )
        v = v + modal_step * acceleration
        return q + modal_step * v, v

    q1, v1 = advance_modes(q0, v0, column_of(total1, MB, MB))
    g2[gx] = stretch_row(q1, v1)
    stage2 = all_gx(g2, 2)
    stage1.wait_send()
    stage2.wait_recv()
    hysteresis, damper_part = response(jnp.sum(g2[...], axis=0), hysteresis)
    damp_o[...] = hysteresis
    h3[gy] = row_of(damper_part)
    stage3 = all_gy(h3, 3)
    stage2.wait_send()
    stage3.wait_recv()
    q2, v2 = advance_modes(q1, v1, column_of(jnp.sum(h3[...], axis=0), MB))
    modal_o[0:1, :] = row_of(q2, 0, MB)
    modal_o[1:2, :] = row_of(v2, 0, MB)
    stage3.wait_send()


def body(
    velocity, pressure, viscosity, wind_profile, panel_area, slot_cell, slot_panel, panel_shapes,
    node_shapes, damper_node, damper_viscous, damper_hysteretic, frequency, damping_ratio,
    modal_state, damper_state,
):
    any_space = pl.BlockSpec(memory_space=pl.ANY)
    vmem = pl.BlockSpec(memory_space=pltpu.VMEM)
    smem = pl.BlockSpec(memory_space=pltpu.SMEM)
    f32, bf16 = jnp.float32, jnp.bfloat16
    slots = slot_panel.shape[1]
    vel, pre, modal, damp = pl.pallas_call(
        kernel,
        out_shape=(
            jax.ShapeDtypeStruct(velocity.shape, f32),
            jax.ShapeDtypeStruct(pressure.shape, f32),
            jax.ShapeDtypeStruct(modal_state.shape, f32),
            jax.ShapeDtypeStruct((1, DB), f32),
        ),
        in_specs=[any_space] * 3 + [vmem] * 2 + [smem] + [vmem] * 11,
        out_specs=(vmem,) * 4,
        scratch_shapes=[
            pltpu.VMEM((4, CX + 2, CY + 16, NZ), f32),
            pltpu.VMEM((4, CX + 2, CY + 16, NZ), f32),
            pltpu.VMEM((CX, CY, NZ), f32),
            pltpu.VMEM((2, 2, 4, CY, NZ), bf16),
            pltpu.VMEM((2, 2, 4, CY, NZ), bf16),
            pltpu.VMEM((2, 2, 4, CX, NZ), f32),
            pltpu.VMEM((2, 2, 4, CX, NZ), f32),
            pltpu.VMEM((SL, NZ), f32),
            pltpu.VMEM((128, slots), bf16),
            pltpu.VMEM((16, slots), bf16),
            pltpu.VMEM((NGX, 2, 128), f32),
            pltpu.VMEM((NGY, 1, 128), f32),
            pltpu.VMEM((NGX, 1, 128), f32),
            pltpu.VMEM((NGY, 1, 128), f32),
            pltpu.SemaphoreType.DMA((3,)),
            pltpu.SemaphoreType.DMA((2, 4)),
            pltpu.SemaphoreType.DMA((2, 4)),
            pltpu.SemaphoreType.DMA((2, 4)),
            pltpu.SemaphoreType.DMA((2, 4)),
            pltpu.SemaphoreType.DMA((4,)),
            pltpu.SemaphoreType.DMA((4,)),
        ],
        compiler_params=pltpu.CompilerParams(
            collective_id=0, has_side_effects=True, vmem_limit_bytes=40 << 20
        ),
    )(
        velocity, pressure, viscosity, wind_profile.reshape(1, -1), panel_area.reshape(1, -1),
        slot_cell, slot_cell, slot_panel.reshape(slots // 128, 128), panel_shapes.T, node_shapes.T,
        damper_node.reshape(1, -1), damper_viscous.reshape(1, -1), damper_hysteretic.reshape(1, -1),
        frequency.reshape(1, -1), damping_ratio.reshape(1, -1), modal_state,
        damper_state.reshape(1, -1),
    )
    return vel, pre, modal, damp.reshape(-1)


def solution(mesh):
    placed = (
        P(None, "gx", "gy", None),
        P("gx", "gy", None),
        P("gx", "gy", None),
        P(),
        P("gy"),
        P("gy", "gx"),
        P("gy", None),
        P("gy", "gx"),
        P(None, "gx"),
        P("gy"),
        P("gy"),
        P("gy"),
        P("gx"),
        P("gx"),
        P(None, "gx"),
        P("gy"),
    )
    return jax.shard_map(
        body,
        mesh=mesh,
        in_specs=placed,
        out_specs=(P(None, "gx", "gy", None), P("gx", "gy", None), P(None, "gx"), P("gy")),
        check_vma=False,
    )
```

```python
import jax
import jax.numpy as jnp
from jax import lax
from jax.experimental import pallas as pl
from jax.experimental.pallas import tpu as pltpu
from jax.sharding import PartitionSpec as P

time_step = 0.1
sound_squared = 1.0
modal_step = 0.5
hysteresis_gain = 1.0
shape_beta = 0.5
shape_gamma = 0.5
spring_rate = 0.5

CX, CY, NZ = 8, 48, 256
NGX, NGY = 64, 8
RX = 4
MB = 32
DB = 64
SL = 64
Y0 = 8
YT = CY // 8


def row_of(column, lane_shift=0, lanes=128):
    n = column.shape[0]
    sub = lax.broadcasted_iota(jnp.int32, (n, lanes), 0)
    lane = lax.broadcasted_iota(jnp.int32, (n, lanes), 1)
    return jnp.sum(jnp.where(lane == sub + lane_shift, column, 0.0), axis=0, keepdims=True)


def column_of(row, n, lane_shift=0):
    lanes = row.shape[1]
    sub = lax.broadcasted_iota(jnp.int32, (n, lanes), 0)
    lane = lax.broadcasted_iota(jnp.int32, (n, lanes), 1)
    zero = jnp.zeros((), row.dtype)
    return jnp.sum(jnp.where(lane == sub + lane_shift, row, zero), axis=1, keepdims=True)


def kernel(
    vel_h, pre_h, vis_h, *refs,
):
    small_h = refs[:14]
    (
        vel_o, pre_o, modal_o, damp_o,
        wind, area, cell_s, cell_v, panels, shapes_t, nodes_t,
        dnode, dvisc, dhyst, freq, ratio, modal, dstate,
        f0, f1, vis, xs, xr, ys, yr, samp, onehot, lhs, g0, h1, g2, h3,
        in_sem, small_sem, xss, xrs, yss, yrs, s_sem, r_sem, known,
    ) = refs[14:]
    gx = lax.axis_index("gx")
    gy = lax.axis_index("gy")
    f32, bf16 = jnp.float32, jnp.bfloat16

    def gx_peer(k):
        return {"gx": lax.rem(gx + k, NGX)}

    def gy_peer(k):
        return {"gy": lax.rem(gy + k, NGY)}

    barrier = pltpu.get_barrier_semaphore()

    plane, ring = gx // RX, lax.rem(gx, RX)

    def z_peer(k):
        return {"gx": lax.rem(plane + k, NGX // RX) * RX + ring}

    def x_peer(k):
        return {"gx": plane * RX + lax.rem(ring + k, RX)}

    nz = NGX // RX
    near = [gx_peer(1), gx_peer(NGX - 1)]
    near += [z_peer(k) for k in (1, nz - 1, 2, nz - 2)]
    near += [x_peer(k) for k in range(1, RX)]
    near += [gy_peer(k) for k in range(1, NGY)]
    for peer in near:
        pl.semaphore_signal(barrier, 1, device_id=peer)

    def tell(i, peers):
        for peer in peers:
            pl.semaphore_signal(known.at[i], 1, device_id=peer)

    cv = pltpu.make_async_copy(vel_h, f0.at[0:3, 1 : 1 + CX, Y0 : Y0 + CY, :], in_sem.at[0])
    cp = pltpu.make_async_copy(pre_h, f0.at[3, 1 : 1 + CX, Y0 : Y0 + CY, :], in_sem.at[1])
    cn = pltpu.make_async_copy(vis_h, vis, in_sem.at[2])
    cv.start()
    cp.start()
    cn.start()
    small = [
        pltpu.make_async_copy(src, dst, small_sem.at[i])
        for i, (src, dst) in enumerate(
            zip(
                small_h,
                (wind, area, cell_s, cell_v, panels, shapes_t, nodes_t,
                 dnode, dvisc, dhyst, freq, ratio, modal, dstate),
            )
        )
    ]
    for c in small:
        c.start()
    cv.wait()
    cp.wait()

    y_order = (1, 0, 2, 3)

    def pack_x(f, p, comps):
        for k in comps:
            xs[p, 0, k] = f[k, CX, Y0 : Y0 + CY, :].astype(bf16)
            xs[p, 1, k] = f[k, 1, Y0 : Y0 + CY, :].astype(bf16)

    def pack_y(f, p, slots):
        for q in slots:
            k = y_order[q]
            for x in range(CX):
                ys[p, 0, q, x : x + 1, :] = f[k, x + 1, Y0 + CY - 1 : Y0 + CY, :]
                ys[p, 1, q, x : x + 1, :] = f[k, x + 1, Y0 : Y0 + 1, :]

    def x_copy(p, part, d, lo, hi):
        i = 2 * part + d
        return pltpu.make_async_remote_copy(
            xs.at[p, d, lo:hi], xr.at[p, d, lo:hi], xss.at[p, i], xrs.at[p, i],
            device_id=gx_peer(1 if d == 0 else NGX - 1),
        )

    def y_copy(p, part, d, lo, hi):
        i = 2 * part + d
        return pltpu.make_async_remote_copy(
            ys.at[p, d, lo:hi], yr.at[p, d, lo:hi], yss.at[p, i], yrs.at[p, i],
            device_id=gy_peer(1 if d == 0 else NGY - 1),
        )

    def unpack_x(f, p, comps):
        for k in comps:
            f[k, 0, Y0 : Y0 + CY, :] = jnp.where(gx == 0, 0.0, xr[p, 0, k].astype(f32))
            f[k, CX + 1, Y0 : Y0 + CY, :] = jnp.where(gx == NGX - 1, 0.0, xr[p, 1, k].astype(f32))

    def unpack_y(f, p, slots):
        for q in slots:
            k = y_order[q]
            for x in range(CX):
                f[k, x + 1, Y0 - 1 : Y0, :] = jnp.where(gy == 0, 0.0, yr[p, 0, q, x : x + 1, :])
                f[k, x + 1, Y0 + CY : Y0 + CY + 1, :] = jnp.where(
                    gy == NGY - 1, 0.0, yr[p, 1, q, x : x + 1, :]
                )

    pack_x(f0, 0, range(4))
    pack_y(f0, 0, range(4))
    pl.semaphore_wait(barrier, len(near))
    tell(0, [z_peer(2), z_peer(nz - 2)])
    hx1 = [x_copy(0, 0, d, 0, 4) for d in range(2)]
    hy1 = [y_copy(0, 0, d, 0, 4) for d in range(2)]
    for c in hy1 + hx1:
        c.start()

    for c in small:
        c.wait()
    dn = dnode[...]
    dn2 = jnp.concatenate([dn, dn], axis=1)
    node_no = lax.broadcasted_iota(jnp.int32, (nodes_t.shape[1], 2 * DB), 0)
    pick = jnp.where(node_no == dn2 + 1, 1.0, jnp.where(node_no == dn2, -1.0, 0.0)).astype(bf16)
    drift = jnp.dot(nodes_t[...], pick, preferred_element_type=f32)
    q0 = column_of(modal[0:1, :], MB)
    v0 = column_of(modal[1:2, :], MB)
    omega = column_of(freq[...], MB)
    zeta = column_of(ratio[...], MB)
    first_half = lax.broadcasted_iota(jnp.int32, (MB, 2 * DB), 1) < DB

    def stretch_row(q, v):
        return jnp.sum(drift * jnp.where(first_half, q, v), axis=0, keepdims=True)

    g0[gx, 1:2, :] = stretch_row(q0, v0)

    def table(i, carry):
        low = panels[pl.ds(i, 1), :] & 127
        sub = lax.broadcasted_iota(jnp.int32, (128, 128), 0)
        onehot[:, pl.ds(pl.multiple_of(i * 128, 128), 128)] = (sub == low).astype(f32).astype(bf16)
        return carry

    lax.fori_loop(0, panels.shape[0], table, 0)
    parity = lax.rem(gx, 2)
    own_ids = column_of(panels[pl.ds(gx // 2, 1), :], SL, SL * parity)
    panel_no = lax.broadcasted_iota(jnp.int32, (SL, area.shape[1]), 1)
    own_area = jnp.sum(jnp.where(panel_no == own_ids, area[...], 0.0), axis=1, keepdims=True)
    own_z = column_of(cell_v[...], SL) & (NZ - 1)
    z_mask = (lax.broadcasted_iota(jnp.int32, (SL, NZ), 1) == own_z)

    lane8 = lax.broadcasted_iota(jnp.int32, (8, NZ), 1)

    def above(v):
        return jnp.where(lane8 == NZ - 1, 0.0, pltpu.roll(v, NZ - 1, 1))

    def below(v):
        return jnp.where(lane8 == 0, 0.0, pltpu.roll(v, 1, 1))

    w_row = jnp.broadcast_to((-0.5 * time_step) * wind[...], (8, NZ))
    half = 0.5 * time_step

    def velocity_tile(f, x, t):
        rows = pl.ds(Y0 + 8 * t, 8)
        rows_m = pl.ds(Y0 + 8 * t - 1, 8)
        rows_p = pl.ds(Y0 + 8 * t + 1, 8)
        nu = time_step * vis[x - 1, 8 * t : 8 * t + 8, :]
        pc = f[3, x, rows, :]
        slope = (
            f[3, x + 1, rows, :] - f[3, x - 1, rows, :],
            f[3, x, rows_p, :] - f[3, x, rows_m, :],
            above(pc) - below(pc),
        )
        out = []
        for k in range(3):
            c = f[k, x, rows, :]
            a, b = f[k, x + 1, rows, :], f[k, x - 1, rows, :]
            r, l = f[k, x, rows_p, :], f[k, x, rows_m, :]
            u, d = above(c), below(c)
            lap = ((a + b) + (r + l)) + ((u + d) - 6.0 * c)
            out.append(c + (w_row * (a - b) + nu * lap - half * slope[k]))
        return out

    def pressure_tile(f, x, t):
        rows = pl.ds(Y0 + 8 * t, 8)
        rows_m = pl.ds(Y0 + 8 * t - 1, 8)
        rows_p = pl.ds(Y0 + 8 * t + 1, 8)
        w = f[2, x, rows, :]
        div = (f[0, x + 1, rows, :] - f[0, x - 1, rows, :]) + (
            (f[1, x, rows_p, :] - f[1, x, rows_m, :]) + (above(w) - below(w))
        )
        return f[3, x, rows, :] - (half * sound_squared) * div

    def first_layer(x, carry):
        for t in range(YT):
            rows = slice(Y0 + 8 * t, Y0 + 8 * t + 8)
            new = velocity_tile(f0, x, t)
            for k in range(3):
                f1[k, x, rows, :] = new[k]
            f1[3, x, rows, :] = pressure_tile(f0, x, t)
        return carry

    cn.wait()
    pl.semaphore_wait(known.at[0], 2)
    tell(1, [z_peer(4), z_peer(nz - 4)])
    for c in hy1:
        c.wait_recv()
    unpack_y(f0, 0, range(4))
    lax.fori_loop(2, CX, first_layer, 0)
    for c in hx1:
        c.wait_recv()
    unpack_x(f0, 0, range(4))
    first_layer(1, 0)
    first_layer(CX, 0)

    pack_x(f1, 1, (0,))
    pack_y(f1, 1, (0,))
    hx2 = [x_copy(1, 0, d, 0, 1) for d in range(2)]
    hy2 = [y_copy(1, 0, d, 0, 1) for d in range(2)]
    for c in hx2 + hy2:
        c.start()
    pack_x(f1, 1, (1, 2, 3))
    pack_y(f1, 1, (1, 2, 3))
    hx3 = [x_copy(1, 1, d, 1, 4) for d in range(2)]
    hy3 = [y_copy(1, 1, d, 1, 4) for d in range(2)]
    for c in hx3 + hy3:
        c.start()
    pl.semaphore_wait(known.at[1], 2)
    tell(2, [x_peer(k) for k in range(1, RX)])
    for c in hx2 + hy2:
        c.wait_recv()
    unpack_x(f1, 1, (0,))
    unpack_y(f1, 1, (0,))

    def second_pressure(x, carry):
        for t in range(YT):
            pre_o[x - 1, 8 * t : 8 * t + 8, :] = pressure_tile(f1, x, t)
        return carry

    lax.fori_loop(1, CX + 1, second_pressure, 0)

    for s in range(SL):
        line = cell_s[0, s] >> 8
        plane = line // CY
        samp[s : s + 1, :] = pre_o[plane, pl.ds(line - plane * CY, 1), :]
    sampled = jnp.sum(jnp.where(z_mask, samp[...], 0.0), axis=1, keepdims=True)
    load = (own_area * sampled).astype(bf16).astype(f32)
    g0[gx, 0:1, :] = row_of(load, SL * parity)

    def all_gx(buf, sem_no):
        def send(k, carry):
            pltpu.make_async_remote_copy(
                buf.at[gx], buf.at[gx], s_sem.at[sem_no], r_sem.at[sem_no], device_id=gx_peer(k)
            ).start()
            return carry

        lax.fori_loop(1, NGX, send, 0)
        most = buf.at[pl.ds(0, NGX - 1)]
        return pltpu.make_async_remote_copy(
            most, most, s_sem.at[sem_no], r_sem.at[sem_no], device_id=gx_peer(1)
        )

    def all_gy(buf, sem_no):
        def send(k, carry):
            pltpu.make_async_remote_copy(
                buf.at[gy], buf.at[gy], s_sem.at[sem_no], r_sem.at[sem_no], device_id=gy_peer(k)
            ).start()
            return carry

        lax.fori_loop(1, NGY, send, 0)
        most = buf.at[pl.ds(0, NGY - 1)]
        return pltpu.make_async_remote_copy(
            most, most, s_sem.at[sem_no], r_sem.at[sem_no], device_id=gy_peer(1)
        )

    pl.semaphore_wait(known.at[2], RX - 1)
    stage0 = all_gx(g0, 0)
    for c in hx3 + hy3:
        c.wait_recv()
    unpack_x(f1, 1, (1, 2, 3))
    unpack_y(f1, 1, (1, 2, 3))

    def second_velocity(x, carry):
        for t in range(YT):
            new = velocity_tile(f1, x, t)
            for k in range(3):
                vel_o[k, x - 1, 8 * t : 8 * t + 8, :] = new[k]
        return carry

    lax.fori_loop(1, CX + 1, second_velocity, 0)
    for c in hx1 + hy1 + hx2 + hy2 + hx3 + hy3:
        c.wait_send()

    stage0.wait_recv()
    sub16 = lax.broadcasted_iota(jnp.int32, (16, 128), 0)
    for i in range(NGX // 2):
        pair = g0[2 * i, 0:1, :] + g0[2 * i + 1, 0:1, :]
        high = panels[i : i + 1, :] >> 7
        lhs[:, i * 128 : (i + 1) * 128] = jnp.where(sub16 == high, pair, 0.0).astype(bf16)
    placed = lax.dot_general(
        lhs[...], onehot[...], (((1,), (1,)), ((), ())), preferred_element_type=f32
    )
    part = jnp.zeros((MB, 128), f32)
    for a in range(16):
        part = part + shapes_t[:, a * 128 : (a + 1) * 128].astype(f32) * placed[a : a + 1, :]
    panel_part = jnp.sum(part, axis=1, keepdims=True)

    def response(total, hysteresis):
        stretch = total[:, 0:DB]
        rate = total[:, DB : 2 * DB]
        hysteresis = hysteresis + modal_step * (
            hysteresis_gain * rate
            - shape_beta * jnp.abs(rate) * hysteresis
            - shape_gamma * rate * jnp.abs(hysteresis)
        )
        force = -(dvisc[...] * rate + spring_rate * stretch + dhyst[...] * hysteresis)
        return hysteresis, jnp.sum(drift[:, 0:DB] * force, axis=1, keepdims=True)

    hysteresis, damper_part = response(jnp.sum(g0[:, 1:2, :], axis=0), dstate[...])
    h1[gy] = row_of(panel_part) + row_of(damper_part, MB)
    stage1 = all_gy(h1, 1)
    stage0.wait_send()
    stage1.wait_recv()
    total1 = jnp.sum(h1[...], axis=0)
    panel_modal = column_of(total1, MB)

    def advance_modes(q, v, damper_load):
        acceleration = (
            panel_modal + damper_load - 2.0 * zeta * omega * v - omega * omega * q
        )
        v = v + modal_step * acceleration
        return q + modal_step * v, v

    q1, v1 = advance_modes(q0, v0, column_of(total1, MB, MB))
    g2[gx] = stretch_row(q1, v1)
    stage2 = all_gx(g2, 2)
    stage1.wait_send()
    stage2.wait_recv()
    hysteresis, damper_part = response(jnp.sum(g2[...], axis=0), hysteresis)
    damp_o[...] = hysteresis
    h3[gy] = row_of(damper_part)
    stage3 = all_gy(h3, 3)
    stage2.wait_send()
    stage3.wait_recv()
    q2, v2 = advance_modes(q1, v1, column_of(jnp.sum(h3[...], axis=0), MB))
    modal_o[0:1, :] = row_of(q2, 0, MB)
    modal_o[1:2, :] = row_of(v2, 0, MB)
    stage3.wait_send()


def write_out(*refs):
    n = len(refs) // 2
    sem = refs[-1]
    copies = [pltpu.make_async_copy(refs[i], refs[n + i], sem.at[i]) for i in range(n)]
    for c in copies:
        c.start()
    for c in copies:
        c.wait()


def body(
    velocity, pressure, viscosity, wind_profile, panel_area, slot_cell, slot_panel, panel_shapes,
    node_shapes, damper_node, damper_viscous, damper_hysteretic, frequency, damping_ratio,
    modal_state, damper_state,
):
    hbm = pl.BlockSpec(memory_space=pltpu.MemorySpace.HBM)
    vmem = pl.BlockSpec(memory_space=pltpu.VMEM)
    f32, bf16 = jnp.float32, jnp.bfloat16
    slots = slot_panel.shape[1]
    small = (
        wind_profile.reshape(1, -1), panel_area.reshape(1, -1),
        slot_cell, slot_cell, slot_panel.reshape(slots // 128, 128), panel_shapes.T, node_shapes.T,
        damper_node.reshape(1, -1), damper_viscous.reshape(1, -1), damper_hysteretic.reshape(1, -1),
        frequency.reshape(1, -1), damping_ratio.reshape(1, -1), modal_state,
        damper_state.reshape(1, -1),
    )
    outs = (
        jax.ShapeDtypeStruct(velocity.shape, f32),
        jax.ShapeDtypeStruct(pressure.shape, f32),
        jax.ShapeDtypeStruct(modal_state.shape, f32),
        jax.ShapeDtypeStruct((1, DB), f32),
    )
    held = [
        (pltpu.SMEM if i == 2 else pltpu.VMEM)(a.shape, a.dtype) for i, a in enumerate(small)
    ]
    results = pl.pallas_call(
        kernel,
        out_shape=outs,
        in_specs=[hbm] * (3 + len(small)),
        out_specs=(vmem,) * 4,
        scratch_shapes=held + [
            pltpu.VMEM((4, CX + 2, CY + 16, NZ), f32),
            pltpu.VMEM((4, CX + 2, CY + 16, NZ), f32),
            pltpu.VMEM((CX, CY, NZ), f32),
            pltpu.VMEM((2, 2, 4, CY, NZ), bf16),
            pltpu.VMEM((2, 2, 4, CY, NZ), bf16),
            pltpu.VMEM((2, 2, 4, CX, NZ), f32),
            pltpu.VMEM((2, 2, 4, CX, NZ), f32),
            pltpu.VMEM((SL, NZ), f32),
            pltpu.VMEM((128, slots), bf16),
            pltpu.VMEM((16, slots), bf16),
            pltpu.VMEM((NGX, 2, 128), f32),
            pltpu.VMEM((NGY, 1, 128), f32),
            pltpu.VMEM((NGX, 1, 128), f32),
            pltpu.VMEM((NGY, 1, 128), f32),
            pltpu.SemaphoreType.DMA((3,)),
            pltpu.SemaphoreType.DMA((len(small),)),
            pltpu.SemaphoreType.DMA((2, 4)),
            pltpu.SemaphoreType.DMA((2, 4)),
            pltpu.SemaphoreType.DMA((2, 4)),
            pltpu.SemaphoreType.DMA((2, 4)),
            pltpu.SemaphoreType.DMA((4,)),
            pltpu.SemaphoreType.DMA((4,)),
            pltpu.SemaphoreType.REGULAR((3,)),
        ],
        compiler_params=pltpu.CompilerParams(
            collective_id=0, has_side_effects=True, vmem_limit_bytes=40 << 20
        ),
    )(*[pltpu.with_memory_space_constraint(a, pltpu.MemorySpace.HBM) for a in (velocity, pressure, viscosity, *small)])
    vel, pre, modal, damp = pl.pallas_call(
        write_out,
        out_shape=outs,
        in_specs=[vmem] * 4,
        out_specs=(hbm,) * 4,
        scratch_shapes=[pltpu.SemaphoreType.DMA((4,))], compiler_params=pltpu.CompilerParams(vmem_limit_bytes=1 << 20),
    )(*results)
    return vel, pre, modal, damp.reshape(-1)


def solution(mesh):
    placed = (
        P(None, "gx", "gy", None),
        P("gx", "gy", None),
        P("gx", "gy", None),
        P(),
        P("gy"),
        P("gy", "gx"),
        P("gy", None),
        P("gy", "gx"),
        P(None, "gx"),
        P("gy"),
        P("gy"),
        P("gy"),
        P("gx"),
        P("gx"),
        P(None, "gx"),
        P("gy"),
    )
    return jax.shard_map(
        body,
        mesh=mesh,
        in_specs=placed,
        out_specs=(P(None, "gx", "gy", None), P("gx", "gy", None), P(None, "gx"), P("gy")),
        check_vma=False,
    )
```

```python
import jax
import jax.numpy as jnp
from jax import lax
from jax.experimental import pallas as pl
from jax.experimental.pallas import tpu as pltpu
from jax.sharding import PartitionSpec as P

time_step = 0.1
sound_squared = 1.0
modal_step = 0.5
hysteresis_gain = 1.0
shape_beta = 0.5
shape_gamma = 0.5
spring_rate = 0.5

CX, CY, NZ = 8, 48, 256
NGX, NGY = 64, 8
RX = 4
MB = 32
DB = 64
SL = 64
Y0 = 8
YT = CY // 8


def row_of(column, lane_shift=0, lanes=128):
    n = column.shape[0]
    sub = lax.broadcasted_iota(jnp.int32, (n, lanes), 0)
    lane = lax.broadcasted_iota(jnp.int32, (n, lanes), 1)
    return jnp.sum(jnp.where(lane == sub + lane_shift, column, 0.0), axis=0, keepdims=True)


def column_of(row, n, lane_shift=0):
    lanes = row.shape[1]
    sub = lax.broadcasted_iota(jnp.int32, (n, lanes), 0)
    lane = lax.broadcasted_iota(jnp.int32, (n, lanes), 1)
    zero = jnp.zeros((), row.dtype)
    return jnp.sum(jnp.where(lane == sub + lane_shift, row, zero), axis=1, keepdims=True)


def twice(row):
    return jnp.concatenate([row, row], axis=1)


def kernel(
    vel_h, pre_h, vis_h, *refs,
):
    small_h = refs[:14]
    (
        vel_o, pre_o, modal_o, damp_o,
        wind, area, cell_s, cell_v, panels, shapes_t, nodes_t,
        dnode, dvisc, dhyst, freq, ratio, modal, dstate,
        f0, f1, vis, xs, xr, ys, yr, samp, onehot, lhs,
        shapes_x, nodes_x, pick_all, drift_x, ring_b, dampers_b, g0, h1, g2, late,
        in_sem, small_sem, xss, xrs, yss, yrs, s_sem, r_sem, known,
    ) = refs[14:]
    gx = lax.axis_index("gx")
    gy = lax.axis_index("gy")
    f32, bf16 = jnp.float32, jnp.bfloat16

    def gx_peer(k):
        return {"gx": lax.rem(gx + k, NGX)}

    def gy_peer(k):
        return {"gy": lax.rem(gy + k, NGY)}

    barrier = pltpu.get_barrier_semaphore()

    plane, ring = gx // RX, lax.rem(gx, RX)

    def z_peer(k):
        return {"gx": lax.rem(plane + k, NGX // RX) * RX + ring}

    def x_peer(k):
        return {"gx": plane * RX + lax.rem(ring + k, RX)}

    nz = NGX // RX
    near = [gx_peer(1), gx_peer(NGX - 1)]
    near += [z_peer(k) for k in (1, nz - 1, 2, nz - 2)]
    near += [x_peer(k) for k in range(1, RX)]
    near += [gy_peer(k) for k in range(1, NGY)]
    ring_peers = [x_peer(k) for k in range(1, RX)]
    for peer in near:
        pl.semaphore_signal(barrier, 1, device_id=peer)

    def tell(i, peers):
        for peer in peers:
            pl.semaphore_signal(known.at[i], 1, device_id=peer)

    cv = pltpu.make_async_copy(vel_h, f0.at[0:3, 1 : 1 + CX, Y0 : Y0 + CY, :], in_sem.at[0])
    cp = pltpu.make_async_copy(pre_h, f0.at[3, 1 : 1 + CX, Y0 : Y0 + CY, :], in_sem.at[1])
    cn = pltpu.make_async_copy(vis_h, vis, in_sem.at[2])
    cv.start()
    cp.start()
    cn.start()
    small = [
        pltpu.make_async_copy(src, dst, small_sem.at[i])
        for i, (src, dst) in enumerate(
            zip(
                small_h,
                (wind, area, cell_s, cell_v, panels, shapes_t, nodes_t,
                 dnode, dvisc, dhyst, freq, ratio, modal, dstate),
            )
        )
    ]
    for c in small:
        c.start()
    cv.wait()
    cp.wait()

    y_order = (1, 0, 2, 3)

    def pack_x(f, p, comps):
        for k in comps:
            xs[p, 0, k] = f[k, CX, Y0 : Y0 + CY, :].astype(bf16)
            xs[p, 1, k] = f[k, 1, Y0 : Y0 + CY, :].astype(bf16)

    def pack_y(f, p, slots):
        for q in slots:
            k = y_order[q]
            for x in range(CX):
                ys[p, 0, q, x : x + 1, :] = f[k, x + 1, Y0 + CY - 1 : Y0 + CY, :]
                ys[p, 1, q, x : x + 1, :] = f[k, x + 1, Y0 : Y0 + 1, :]

    def x_copy(p, part, d, lo, hi):
        i = 2 * part + d
        return pltpu.make_async_remote_copy(
            xs.at[p, d, lo:hi], xr.at[p, d, lo:hi], xss.at[p, i], xrs.at[p, i],
            device_id=gx_peer(1 if d == 0 else NGX - 1),
        )

    def y_copy(p, part, d, lo, hi):
        i = 2 * part + d
        return pltpu.make_async_remote_copy(
            ys.at[p, d, lo:hi], yr.at[p, d, lo:hi], yss.at[p, i], yrs.at[p, i],
            device_id=gy_peer(1 if d == 0 else NGY - 1),
        )

    def unpack_x(f, p, comps):
        for k in comps:
            f[k, 0, Y0 : Y0 + CY, :] = jnp.where(gx == 0, 0.0, xr[p, 0, k].astype(f32))
            f[k, CX + 1, Y0 : Y0 + CY, :] = jnp.where(gx == NGX - 1, 0.0, xr[p, 1, k].astype(f32))

    def unpack_y(f, p, slots):
        for q in slots:
            k = y_order[q]
            for x in range(CX):
                f[k, x + 1, Y0 - 1 : Y0, :] = jnp.where(gy == 0, 0.0, yr[p, 0, q, x : x + 1, :])
                f[k, x + 1, Y0 + CY : Y0 + CY + 1, :] = jnp.where(
                    gy == NGY - 1, 0.0, yr[p, 1, q, x : x + 1, :]
                )

    pack_x(f0, 0, range(4))
    pack_y(f0, 0, range(4))
    pl.semaphore_wait(barrier, len(near))
    tell(0, [z_peer(2), z_peer(nz - 2)] + ring_peers)
    hx1 = [x_copy(0, 0, d, 0, 4) for d in range(2)]
    hy1 = [y_copy(0, 0, d, 0, 4) for d in range(2)]
    for c in hy1 + hx1:
        c.start()

    for c in small:
        c.wait()
    dn = dnode[...].astype(f32)
    dn2 = twice(dn)
    node_no = lax.broadcasted_iota(jnp.int32, (nodes_t.shape[1], 2 * DB), 0).astype(f32)

    def pick(row):
        return jnp.where(node_no == row + 1.0, 1.0, jnp.where(node_no == row, -1.0, 0.0)).astype(bf16)

    drift = jnp.dot(nodes_t[...], pick(dn2), preferred_element_type=f32)
    q0 = column_of(modal[0:1, :], MB)
    v0 = column_of(modal[1:2, :], MB)
    first_half = lax.broadcasted_iota(jnp.int32, (MB, 2 * DB), 1) < DB
    odd = lax.rem(gy, 2)
    own_half = (lax.broadcasted_iota(jnp.int32, (1, 2 * DB), 1) // DB) == odd

    def placed_half(row):
        return jnp.where(own_half, twice(row), 0.0)

    dampers_b[gy, 0:1, :] = placed_half(dvisc[...])
    dampers_b[gy, 1:2, :] = placed_half(dhyst[...])
    dampers_b[gy, 2:3, :] = placed_half(dn)
    ring_b[ring, 0:1, :] = jnp.sum(
        drift * jnp.where(first_half, q0, v0), axis=0, keepdims=True
    )
    ring_b[ring, 1:2, :] = row_of(q0, MB * ring)
    ring_b[ring, 2:3, :] = row_of(v0, MB * ring)
    ring_b[ring, 3:4, :] = row_of(column_of(freq[...], MB), MB * ring)
    ring_b[ring, 4:5, :] = row_of(column_of(ratio[...], MB), MB * ring)

    def spread(buf, me, count, sem_no, peer):
        def send(k, carry):
            pltpu.make_async_remote_copy(
                buf.at[me], buf.at[me], s_sem.at[sem_no], r_sem.at[sem_no], device_id=peer(k)
            ).start()
            return carry

        lax.fori_loop(1, count, send, 0)
        most = buf.at[pl.ds(0, count - 1)]
        return pltpu.make_async_remote_copy(
            most, most, s_sem.at[sem_no], r_sem.at[sem_no], device_id=peer(1)
        )

    ring_stage = spread(ring_b, ring, RX, 0, x_peer)
    damper_stage = spread(dampers_b, gy, NGY, 1, gy_peer)

    def table(i, carry):
        low = panels[pl.ds(2 * i + ring // 2, 1), :] & 127
        sub = lax.broadcasted_iota(jnp.int32, (128, 128), 0)
        onehot[:, pl.ds(pl.multiple_of(i * 128, 128), 128)] = (sub == low).astype(f32).astype(bf16)
        return carry

    lax.fori_loop(0, nz, table, 0)
    shapes_x[ring] = shapes_t[...]
    nodes_x[ring] = nodes_t[...]
    parity = lax.rem(gx, 2)
    own_ids = column_of(panels[pl.ds(gx // 2, 1), :], SL, SL * parity)
    panel_no = lax.broadcasted_iota(jnp.int32, (SL, area.shape[1]), 1)
    own_area = jnp.sum(jnp.where(panel_no == own_ids, area[...], 0.0), axis=1, keepdims=True)
    own_z = column_of(cell_v[...], SL) & (NZ - 1)
    z_mask = (lax.broadcasted_iota(jnp.int32, (SL, NZ), 1) == own_z)

    lane8 = lax.broadcasted_iota(jnp.int32, (8, NZ), 1)

    def above(v):
        return jnp.where(lane8 == NZ - 1, 0.0, pltpu.roll(v, NZ - 1, 1))

    def below(v):
        return jnp.where(lane8 == 0, 0.0, pltpu.roll(v, 1, 1))

    w_row = jnp.broadcast_to((-0.5 * time_step) * wind[...], (8, NZ))
    half = 0.5 * time_step

    def velocity_tile(f, x, t):
        rows = pl.ds(Y0 + 8 * t, 8)
        rows_m = pl.ds(Y0 + 8 * t - 1, 8)
        rows_p = pl.ds(Y0 + 8 * t + 1, 8)
        nu = time_step * vis[x - 1, 8 * t : 8 * t + 8, :]
        pc = f[3, x, rows, :]
        slope = (
            f[3, x + 1, rows, :] - f[3, x - 1, rows, :],
            f[3, x, rows_p, :] - f[3, x, rows_m, :],
            above(pc) - below(pc),
        )
        out = []
        for k in range(3):
            c = f[k, x, rows, :]
            a, b = f[k, x + 1, rows, :], f[k, x - 1, rows, :]
            r, l = f[k, x, rows_p, :], f[k, x, rows_m, :]
            u, d = above(c), below(c)
            lap = ((a + b) + (r + l)) + ((u + d) - 6.0 * c)
            out.append(c + (w_row * (a - b) + nu * lap - half * slope[k]))
        return out

    def pressure_tile(f, x, t):
        rows = pl.ds(Y0 + 8 * t, 8)
        rows_m = pl.ds(Y0 + 8 * t - 1, 8)
        rows_p = pl.ds(Y0 + 8 * t + 1, 8)
        w = f[2, x, rows, :]
        div = (f[0, x + 1, rows, :] - f[0, x - 1, rows, :]) + (
            (f[1, x, rows_p, :] - f[1, x, rows_m, :]) + (above(w) - below(w))
        )
        return f[3, x, rows, :] - (half * sound_squared) * div

    def first_layer(x, carry):
        for t in range(YT):
            rows = slice(Y0 + 8 * t, Y0 + 8 * t + 8)
            new = velocity_tile(f0, x, t)
            for k in range(3):
                f1[k, x, rows, :] = new[k]
            f1[3, x, rows, :] = pressure_tile(f0, x, t)
        return carry

    cn.wait()
    pl.semaphore_wait(known.at[0], 2 + len(ring_peers))
    tell(1, [z_peer(4), z_peer(nz - 4)])
    for c in hy1:
        c.wait_recv()
    unpack_y(f0, 0, range(4))
    lax.fori_loop(2, CX, first_layer, 0)
    for c in hx1:
        c.wait_recv()
    unpack_x(f0, 0, range(4))
    first_layer(1, 0)
    first_layer(CX, 0)

    pack_x(f1, 1, (0,))
    pack_y(f1, 1, (0,))
    hx2 = [x_copy(1, 0, d, 0, 1) for d in range(2)]
    hy2 = [y_copy(1, 0, d, 0, 1) for d in range(2)]
    for c in hx2 + hy2:
        c.start()
    shapes_stage = spread(shapes_x, ring, RX, 2, x_peer)
    pack_x(f1, 1, (1, 2, 3))
    pack_y(f1, 1, (1, 2, 3))
    hx3 = [x_copy(1, 1, d, 1, 4) for d in range(2)]
    hy3 = [y_copy(1, 1, d, 1, 4) for d in range(2)]
    for c in hx3 + hy3:
        c.start()
    for c in hx2 + hy2:
        c.wait_recv()
    unpack_x(f1, 1, (0,))
    unpack_y(f1, 1, (0,))

    def second_pressure(x, carry):
        for t in range(YT):
            pre_o[x - 1, 8 * t : 8 * t + 8, :] = pressure_tile(f1, x, t)
        return carry

    lax.fori_loop(1, CX + 1, second_pressure, 0)

    for s in range(SL):
        line = cell_s[0, s] >> 8
        layer = line // CY
        samp[s : s + 1, :] = pre_o[layer, pl.ds(line - layer * CY, 1), :]
    sampled = jnp.sum(jnp.where(z_mask, samp[...], 0.0), axis=1, keepdims=True)
    load = (own_area * sampled).astype(bf16).astype(f32)
    g0[plane, 0:1, :] = row_of(load, SL * parity)
    ring_stage.wait_recv()
    g0[plane, 1:2, :] = jnp.sum(ring_b[:, 0:1, :], axis=0)
    pl.semaphore_wait(known.at[1], 2)
    stage0 = spread(g0, plane, nz, 3, z_peer)
    nodes_stage = spread(nodes_x, ring, RX, 4, x_peer)
    for c in hx3 + hy3:
        c.wait_recv()
    unpack_x(f1, 1, (1, 2, 3))
    unpack_y(f1, 1, (1, 2, 3))

    def second_velocity(x, carry):
        for t in range(YT):
            new = velocity_tile(f1, x, t)
            for k in range(3):
                vel_o[k, x - 1, 8 * t : 8 * t + 8, :] = new[k]
        return carry

    lax.fori_loop(1, CX + 1, second_velocity, 0)
    for c in hx1 + hy1 + hx2 + hy2 + hx3 + hy3 + [ring_stage, damper_stage]:
        c.wait_send()
    damper_stage.wait_recv()

    def paired(buf, row):
        return jnp.concatenate(
            [buf[2 * j, row : row + 1, :] + buf[2 * j + 1, row : row + 1, :] for j in range(NGY // 2)],
            axis=0,
        )

    visc_all, hyst_all, node_all = (paired(dampers_b, r) for r in range(3))
    for j in range(NGY // 2):
        pick_all[:, j * 128 : (j + 1) * 128] = pick(node_all[j : j + 1, :])
    q0_row, v0_row, omega, zeta = (jnp.sum(ring_b[:, r : r + 1, :], axis=0) for r in range(1, 5))

    shapes_stage.wait_recv()
    stage0.wait_recv()
    sub16 = lax.broadcasted_iota(jnp.int32, (16, 128), 0)
    for i in range(nz):
        high = panels[pl.ds(2 * i + ring // 2, 1), :] >> 7
        lhs[:, i * 128 : (i + 1) * 128] = jnp.where(sub16 == high, g0[i, 0:1, :], 0.0).astype(bf16)
    placed = lax.dot_general(
        lhs[...], onehot[...], (((1,), (1,)), ((), ())), preferred_element_type=f32
    )
    parts = []
    for r in range(RX):
        part = jnp.zeros((MB, 128), f32)
        for a in range(16):
            part = part + shapes_x[r, :, a * 128 : (a + 1) * 128].astype(f32) * placed[a : a + 1, :]
        parts.append(row_of(jnp.sum(part, axis=1, keepdims=True), MB * r))

    def response(stretch, rate, viscous, hysteretic, hysteresis):
        hysteresis = hysteresis + modal_step * (
            hysteresis_gain * rate
            - shape_beta * jnp.abs(rate) * hysteresis
            - shape_gamma * rate * jnp.abs(hysteresis)
        )
        return hysteresis, -(viscous * rate + spring_rate * stretch + hysteretic * hysteresis)

    first = jnp.sum(g0[:, 1:2, :], axis=0)
    stretch0 = first[:, 0:DB]
    hysteresis, force = response(stretch0, first[:, DB : 2 * DB], dvisc[...], dhyst[...], dstate[...])
    damper_part = jnp.sum(drift[:, 0:DB] * force, axis=1, keepdims=True)
    spot = ring * NGY + gy
    h1[spot, 0:1, :] = (parts[0] + parts[1]) + (parts[2] + parts[3])
    h1[spot, 1:2, :] = row_of(damper_part, MB * ring)
    h1[spot, 2:3, :] = placed_half(stretch0)
    h1[spot, 3:4, :] = placed_half(hysteresis)

    def plane_peer(k):
        there = lax.rem(spot + k, RX * NGY)
        return {"gx": plane * RX + there // NGY, "gy": lax.rem(there, NGY)}

    stage1 = spread(h1, spot, RX * NGY, 5, plane_peer)
    stage0.wait_send()
    shapes_stage.wait_send()
    nodes_stage.wait_recv()
    for r in range(RX):
        drift_x[r * MB : (r + 1) * MB, :] = jnp.dot(
            nodes_x[r], pick_all[...], preferred_element_type=f32
        )
    nodes_stage.wait_send()
    stage1.wait_recv()
    panel_modal = jnp.sum(h1[:, 0:1, :], axis=0)
    damper_modal = jnp.sum(h1[:, 1:2, :], axis=0)
    stretch_all, hysteresis_all = paired(h1, 2), paired(h1, 3)

    def advance_modes(q, v, damper_load):
        acceleration = (
            panel_modal + damper_load - 2.0 * zeta * omega * v - omega * omega * q
        )
        v = v + modal_step * acceleration
        return q + modal_step * v, v

    q1, v1 = advance_modes(q0_row, v0_row, damper_modal)
    v1_column = column_of(v1, RX * MB)
    for j in range(NGY // 2):
        g2[plane, j : j + 1, :] = jnp.sum(
            drift_x[:, j * 128 : (j + 1) * 128] * v1_column, axis=0, keepdims=True
        )
    stage2 = spread(g2, plane, nz, 6, z_peer)
    stage1.wait_send()
    stage2.wait_recv()
    rate_all = jnp.sum(g2[...], axis=0)
    stretch_all = stretch_all + modal_step * rate_all
    hysteresis_all, force = response(stretch_all, rate_all, visc_all, hyst_all, hysteresis_all)
    late[...] = hysteresis_all
    own = late[pl.ds(gy // 2, 1), :]
    damp_o[...] = jnp.where(odd == 1, own[:, DB : 2 * DB], own[:, 0:DB])
    part = jnp.zeros((MB, 128), f32)
    for j in range(NGY // 2):
        rows = pl.ds(pl.multiple_of(ring * MB, MB), MB)
        part = part + drift_x[rows, j * 128 : (j + 1) * 128] * force[j : j + 1, :]
    damper_modal = row_of(jnp.sum(part, axis=1, keepdims=True), MB * ring)
    q2, v2 = advance_modes(q1, v1, damper_modal)
    modal_o[0:1, :] = row_of(column_of(q2, MB, MB * ring), 0, MB)
    modal_o[1:2, :] = row_of(column_of(v2, MB, MB * ring), 0, MB)
    stage2.wait_send()


def write_out(*refs):
    n = len(refs) // 2
    sem = refs[-1]
    copies = [pltpu.make_async_copy(refs[i], refs[n + i], sem.at[i]) for i in range(n)]
    for c in copies:
        c.start()
    for c in copies:
        c.wait()


def body(
    velocity, pressure, viscosity, wind_profile, panel_area, slot_cell, slot_panel, panel_shapes,
    node_shapes, damper_node, damper_viscous, damper_hysteretic, frequency, damping_ratio,
    modal_state, damper_state,
):
    hbm = pl.BlockSpec(memory_space=pltpu.MemorySpace.HBM)
    vmem = pl.BlockSpec(memory_space=pltpu.VMEM)
    f32, bf16 = jnp.float32, jnp.bfloat16
    slots = slot_panel.shape[1]
    small = (
        wind_profile.reshape(1, -1), panel_area.reshape(1, -1),
        slot_cell, slot_cell, slot_panel.reshape(slots // 128, 128), panel_shapes.T, node_shapes.T,
        damper_node.reshape(1, -1), damper_viscous.reshape(1, -1), damper_hysteretic.reshape(1, -1),
        frequency.reshape(1, -1), damping_ratio.reshape(1, -1), modal_state,
        damper_state.reshape(1, -1),
    )
    outs = (
        jax.ShapeDtypeStruct(velocity.shape, f32),
        jax.ShapeDtypeStruct(pressure.shape, f32),
        jax.ShapeDtypeStruct(modal_state.shape, f32),
        jax.ShapeDtypeStruct((1, DB), f32),
    )
    held = [
        (pltpu.SMEM if i == 2 else pltpu.VMEM)(a.shape, a.dtype) for i, a in enumerate(small)
    ]
    results = pl.pallas_call(
        kernel,
        out_shape=outs,
        in_specs=[hbm] * (3 + len(small)),
        out_specs=(vmem,) * 4,
        scratch_shapes=held + [
            pltpu.VMEM((4, CX + 2, CY + 16, NZ), f32),
            pltpu.VMEM((4, CX + 2, CY + 16, NZ), f32),
            pltpu.VMEM((CX, CY, NZ), f32),
            pltpu.VMEM((2, 2, 4, CY, NZ), bf16),
            pltpu.VMEM((2, 2, 4, CY, NZ), bf16),
            pltpu.VMEM((2, 2, 4, CX, NZ), f32),
            pltpu.VMEM((2, 2, 4, CX, NZ), f32),
            pltpu.VMEM((SL, NZ), f32),
            pltpu.VMEM((128, NGX // RX * 128), bf16),
            pltpu.VMEM((16, NGX // RX * 128), bf16),
            pltpu.VMEM((RX,) + panel_shapes.shape[::-1], bf16),
            pltpu.VMEM((RX,) + node_shapes.shape[::-1], bf16),
            pltpu.VMEM((node_shapes.shape[0], DB * NGY), bf16),
            pltpu.VMEM((RX * MB, DB * NGY), f32),
            pltpu.VMEM((RX, 8, 128), f32),
            pltpu.VMEM((NGY, 4, 128), f32),
            pltpu.VMEM((NGX // RX, 2, 128), f32),
            pltpu.VMEM((RX * NGY, 4, 128), f32),
            pltpu.VMEM((NGX // RX, NGY // 2, 128), f32),
            pltpu.VMEM((NGY // 2, 128), f32),
            pltpu.SemaphoreType.DMA((3,)),
            pltpu.SemaphoreType.DMA((len(small),)),
            pltpu.SemaphoreType.DMA((2, 4)),
            pltpu.SemaphoreType.DMA((2, 4)),
            pltpu.SemaphoreType.DMA((2, 4)),
            pltpu.SemaphoreType.DMA((2, 4)),
            pltpu.SemaphoreType.DMA((7,)),
            pltpu.SemaphoreType.DMA((7,)),
            pltpu.SemaphoreType.REGULAR((2,)),
        ],
        compiler_params=pltpu.CompilerParams(
            collective_id=0, has_side_effects=True, vmem_limit_bytes=40 << 20
        ),
    )(*[pltpu.with_memory_space_constraint(a, pltpu.MemorySpace.HBM) for a in (velocity, pressure, viscosity, *small)])
    vel, pre, modal, damp = pl.pallas_call(
        write_out,
        out_shape=outs,
        in_specs=[vmem] * 4,
        out_specs=(hbm,) * 4,
        scratch_shapes=[pltpu.SemaphoreType.DMA((4,))], compiler_params=pltpu.CompilerParams(vmem_limit_bytes=1 << 20),
    )(*results)
    return vel, pre, modal, damp.reshape(-1)


def solution(mesh):
    placed = (
        P(None, "gx", "gy", None),
        P("gx", "gy", None),
        P("gx", "gy", None),
        P(),
        P("gy"),
        P("gy", "gx"),
        P("gy", None),
        P("gy", "gx"),
        P(None, "gx"),
        P("gy"),
        P("gy"),
        P("gy"),
        P("gx"),
        P("gx"),
        P(None, "gx"),
        P("gy"),
    )
    return jax.shard_map(
        body,
        mesh=mesh,
        in_specs=placed,
        out_specs=(P(None, "gx", "gy", None), P("gx", "gy", None), P(None, "gx"), P("gy")),
        check_vma=False,
    )
```

```python
import jax
import jax.numpy as jnp
from jax import lax
from jax.experimental import pallas as pl
from jax.experimental.pallas import tpu as pltpu
from jax.sharding import PartitionSpec as P

time_step = 0.1
sound_squared = 1.0
modal_step = 0.5
hysteresis_gain = 1.0
shape_beta = 0.5
shape_gamma = 0.5
spring_rate = 0.5

CX, CY, NZ = 8, 48, 256
NGX, NGY = 64, 8
RX = 4
MB = 32
DB = 64
SL = 64
Y0 = 8
YT = CY // 8


def row_of(column, lane_shift=0, lanes=128):
    n = column.shape[0]
    sub = lax.broadcasted_iota(jnp.int32, (n, lanes), 0)
    lane = lax.broadcasted_iota(jnp.int32, (n, lanes), 1)
    return jnp.sum(jnp.where(lane == sub + lane_shift, column, 0.0), axis=0, keepdims=True)


def column_of(row, n, lane_shift=0):
    lanes = row.shape[1]
    sub = lax.broadcasted_iota(jnp.int32, (n, lanes), 0)
    lane = lax.broadcasted_iota(jnp.int32, (n, lanes), 1)
    zero = jnp.zeros((), row.dtype)
    return jnp.sum(jnp.where(lane == sub + lane_shift, row, zero), axis=1, keepdims=True)


def twice(row):
    return jnp.concatenate([row, row], axis=1)


def kernel(
    vel_h, pre_h, vis_h, *refs,
):
    small_h = refs[:14]
    (
        vel_o, pre_o, modal_o, damp_o,
        wind, area, cell_s, cell_v, panels, shapes_t, nodes_t,
        dnode, dvisc, dhyst, freq, ratio, modal, dstate,
        f0, f1, vis, xs, xr, ys, yr, yi, cs, cr, samp, onehot, lhs,
        shapes_x, nodes_x, pick_all, drift_x, ring_b, dampers_b, g0, h1, g2, late,
        in_sem, small_sem, xss, xrs, yss, yrs, css, crs, s_sem, r_sem, known,
    ) = refs[14:]
    gx = lax.axis_index("gx")
    gy = lax.axis_index("gy")
    f32, bf16 = jnp.float32, jnp.bfloat16

    def gx_peer(k):
        return {"gx": lax.rem(gx + k, NGX)}

    def gy_peer(k):
        return {"gy": lax.rem(gy + k, NGY)}

    barrier = pltpu.get_barrier_semaphore()

    plane, ring = gx // RX, lax.rem(gx, RX)

    def z_peer(k):
        return {"gx": lax.rem(plane + k, NGX // RX) * RX + ring}

    def x_peer(k):
        return {"gx": plane * RX + lax.rem(ring + k, RX)}

    nz = NGX // RX
    near = [gx_peer(1), gx_peer(NGX - 1)]
    near += [z_peer(k) for k in (1, nz - 1, 2, nz - 2)]
    near += [x_peer(k) for k in range(1, RX)]
    near += [gy_peer(k) for k in range(1, NGY)]
    ring_peers = [x_peer(k) for k in range(1, RX)]
    for peer in near:
        pl.semaphore_signal(barrier, 1, device_id=peer)

    def tell(i, peers):
        for peer in peers:
            pl.semaphore_signal(known.at[i], 1, device_id=peer)

    cv = pltpu.make_async_copy(vel_h, f0.at[0:3, 1 : 1 + CX, Y0 : Y0 + CY, :], in_sem.at[0])
    cp = pltpu.make_async_copy(pre_h, f0.at[3, 1 : 1 + CX, Y0 : Y0 + CY, :], in_sem.at[1])
    cn = pltpu.make_async_copy(vis_h, vis, in_sem.at[2])
    cv.start()
    cp.start()
    cn.start()
    small = [
        pltpu.make_async_copy(src, dst, small_sem.at[i])
        for i, (src, dst) in enumerate(
            zip(
                small_h,
                (wind, area, cell_s, cell_v, panels, shapes_t, nodes_t,
                 dnode, dvisc, dhyst, freq, ratio, modal, dstate),
            )
        )
    ]
    for c in small:
        c.start()
    cv.wait()
    cp.wait()

    y_order = (1, 0, 2, 3)

    def pack_x(f, p, comps):
        for k in comps:
            xs[p, 0, k] = f[k, CX, Y0 : Y0 + CY, :].astype(bf16)
            xs[p, 1, k] = f[k, 1, Y0 : Y0 + CY, :].astype(bf16)

    def pack_y(f, p, slots):
        for q in slots:
            k = y_order[q]
            for x in range(CX):
                ys[p, 0, q, x : x + 1, :] = f[k, x + 1, Y0 + CY - 1 : Y0 + CY, :]
                ys[p, 1, q, x : x + 1, :] = f[k, x + 1, Y0 : Y0 + 1, :]

    def x_copy(p, part, d, lo, hi):
        i = 2 * part + d
        return pltpu.make_async_remote_copy(
            xs.at[p, d, lo:hi], xr.at[p, d, lo:hi], xss.at[p, i], xrs.at[p, i],
            device_id=gx_peer(1 if d == 0 else NGX - 1),
        )

    def y_copy(p, part, d, lo, hi):
        i = 2 * part + d
        return pltpu.make_async_remote_copy(
            ys.at[p, d, lo:hi], yr.at[p, d, lo:hi], yss.at[p, i], yrs.at[p, i],
            device_id=gy_peer(1 if d == 0 else NGY - 1),
        )

    def unpack_x(f, p, comps):
        for k in comps:
            f[k, 0, Y0 : Y0 + CY, :] = jnp.where(gx == 0, 0.0, xr[p, 0, k].astype(f32))
            f[k, CX + 1, Y0 : Y0 + CY, :] = jnp.where(gx == NGX - 1, 0.0, xr[p, 1, k].astype(f32))

    def unpack_y(f, p, slots):
        for q in slots:
            k = y_order[q]
            for x in range(CX):
                f[k, x + 1, Y0 - 1 : Y0, :] = jnp.where(gy == 0, 0.0, yr[p, 0, q, x : x + 1, :])
                f[k, x + 1, Y0 + CY : Y0 + CY + 1, :] = jnp.where(
                    gy == NGY - 1, 0.0, yr[p, 1, q, x : x + 1, :]
                )

    lane8 = lax.broadcasted_iota(jnp.int32, (8, NZ), 1)

    def above(v):
        return jnp.where(lane8 == NZ - 1, 0.0, pltpu.roll(v, NZ - 1, 1))

    def below(v):
        return jnp.where(lane8 == 0, 0.0, pltpu.roll(v, 1, 1))

    small[0].wait()
    w_row = jnp.broadcast_to((-0.5 * time_step) * wind[...], (8, NZ))
    half = 0.5 * time_step

    x8 = lax.broadcasted_iota(jnp.int32, (CX, NZ), 0)

    def next_x(v):
        return jnp.where(x8 == CX - 1, 0.0, pltpu.roll(v, CX - 1, 0))

    def last_x(v):
        return jnp.where(x8 == 0, 0.0, pltpu.roll(v, 1, 0))

    def outer_x(d):
        x, inner, sign = (CX, CX - 1, 1.0) if d == 0 else (1, 2, -1.0)
        zero = jnp.zeros((1, NZ), f32)
        f0[0, x, Y0 - 1 : Y0, :] = zero
        f0[0, x, Y0 + CY : Y0 + CY + 1, :] = zero
        for t in range(YT):
            rows = pl.ds(Y0 + 8 * t, 8)
            own = slice(8 * t, 8 * t + 8)
            c, i, p = f0[0, x, rows, :], f0[0, inner, rows, :], f0[3, inner, rows, :]
            r, l = f0[0, x, pl.ds(Y0 + 8 * t + 1, 8), :], f0[0, x, pl.ds(Y0 + 8 * t - 1, 8), :]
            lap = (i + (r + l)) + ((above(c) + below(c)) - 6.0 * c)
            nu = time_step * vis[x - 1, own, :]
            tile = c + (nu * lap + sign * (half * p - w_row * i))
            yield own, tile, vis[x - 1, own, :]

    def pack_outer_x():
        for d in range(2):
            for own, tile, nu in outer_x(d):
                xs[0, d, 4, own, :] = tile.astype(bf16)
                xs[0, d, 5, own, :] = nu.astype(bf16)

    def pack_outer_y():
        for d in range(2):
            y, inner, sign = (Y0 + CY - 1, Y0 + CY - 2, 1.0) if d == 0 else (Y0, Y0 + 1, -1.0)
            for x in range(CX):
                yi[d, 0, x : x + 1, :] = f0[1, x + 1, inner : inner + 1, :]
                yi[d, 1, x : x + 1, :] = f0[3, x + 1, inner : inner + 1, :]
                ys[0, d, 5, x : x + 1, :] = vis[x, y - Y0 : y - Y0 + 1, :]
            c, nu = ys[0, d, 0], time_step * ys[0, d, 5]
            a, b = next_x(c), last_x(c)
            lap = (yi[d, 0] + (a + b)) + ((above(c) + below(c)) - 6.0 * c)
            ys[0, d, 4] = c + (w_row * (a - b) + nu * lap + (sign * half) * yi[d, 1])

    pack_y(f0, 0, range(4))
    cn.wait()
    pack_outer_y()
    pack_x(f0, 0, range(4))
    pack_outer_x()
    pl.semaphore_wait(barrier, len(near))
    tell(0, [z_peer(2), z_peer(nz - 2)] + ring_peers)
    hx1 = [x_copy(0, 0, d, 0, 6) for d in range(2)]
    hy1 = [y_copy(0, 0, d, 0, 6) for d in range(2)]
    for c in hy1 + hx1:
        c.start()

    for c in small[1:]:
        c.wait()
    dn = dnode[...].astype(f32)
    dn2 = twice(dn)
    node_no = lax.broadcasted_iota(jnp.int32, (nodes_t.shape[1], 2 * DB), 0).astype(f32)

    def pick(row):
        return jnp.where(node_no == row + 1.0, 1.0, jnp.where(node_no == row, -1.0, 0.0)).astype(bf16)

    drift = jnp.dot(nodes_t[...], pick(dn2), preferred_element_type=f32)
    q0 = column_of(modal[0:1, :], MB)
    v0 = column_of(modal[1:2, :], MB)
    first_half = lax.broadcasted_iota(jnp.int32, (MB, 2 * DB), 1) < DB
    odd = lax.rem(gy, 2)
    own_half = (lax.broadcasted_iota(jnp.int32, (1, 2 * DB), 1) // DB) == odd

    def placed_half(row):
        return jnp.where(own_half, twice(row), 0.0)

    dampers_b[gy, 0:1, :] = placed_half(dvisc[...])
    dampers_b[gy, 1:2, :] = placed_half(dhyst[...])
    dampers_b[gy, 2:3, :] = placed_half(dn)
    ring_b[ring, 0:1, :] = jnp.sum(
        drift * jnp.where(first_half, q0, v0), axis=0, keepdims=True
    )
    ring_b[ring, 1:2, :] = row_of(q0, MB * ring)
    ring_b[ring, 2:3, :] = row_of(v0, MB * ring)
    ring_b[ring, 3:4, :] = row_of(column_of(freq[...], MB), MB * ring)
    ring_b[ring, 4:5, :] = row_of(column_of(ratio[...], MB), MB * ring)

    def spread(buf, me, count, sem_no, peer):
        def send(k, carry):
            pltpu.make_async_remote_copy(
                buf.at[me], buf.at[me], s_sem.at[sem_no], r_sem.at[sem_no], device_id=peer(k)
            ).start()
            return carry

        lax.fori_loop(1, count, send, 0)
        most = buf.at[pl.ds(0, count - 1)]
        return pltpu.make_async_remote_copy(
            most, most, s_sem.at[sem_no], r_sem.at[sem_no], device_id=peer(1)
        )

    ring_stage = spread(ring_b, ring, RX, 0, x_peer)
    damper_stage = spread(dampers_b, gy, NGY, 1, gy_peer)

    parity = lax.rem(gx, 2)
    own_ids = column_of(panels[pl.ds(gx // 2, 1), :], SL, SL * parity)
    panel_no = lax.broadcasted_iota(jnp.int32, (SL, area.shape[1]), 1)
    own_area = jnp.sum(jnp.where(panel_no == own_ids, area[...], 0.0), axis=1, keepdims=True)
    own_z = column_of(cell_v[...], SL) & (NZ - 1)
    z_mask = (lax.broadcasted_iota(jnp.int32, (SL, NZ), 1) == own_z)

    def velocity_tile(f, x, t):
        rows = pl.ds(Y0 + 8 * t, 8)
        rows_m = pl.ds(Y0 + 8 * t - 1, 8)
        rows_p = pl.ds(Y0 + 8 * t + 1, 8)
        nu = time_step * vis[x - 1, 8 * t : 8 * t + 8, :]
        pc = f[3, x, rows, :]
        slope = (
            f[3, x + 1, rows, :] - f[3, x - 1, rows, :],
            f[3, x, rows_p, :] - f[3, x, rows_m, :],
            above(pc) - below(pc),
        )
        out = []
        for k in range(3):
            c = f[k, x, rows, :]
            a, b = f[k, x + 1, rows, :], f[k, x - 1, rows, :]
            r, l = f[k, x, rows_p, :], f[k, x, rows_m, :]
            u, d = above(c), below(c)
            lap = ((a + b) + (r + l)) + ((u + d) - 6.0 * c)
            out.append(c + (w_row * (a - b) + nu * lap - half * slope[k]))
        return out

    def pressure_tile(f, x, t):
        rows = pl.ds(Y0 + 8 * t, 8)
        rows_m = pl.ds(Y0 + 8 * t - 1, 8)
        rows_p = pl.ds(Y0 + 8 * t + 1, 8)
        w = f[2, x, rows, :]
        div = (f[0, x + 1, rows, :] - f[0, x - 1, rows, :]) + (
            (f[1, x, rows_p, :] - f[1, x, rows_m, :]) + (above(w) - below(w))
        )
        return f[3, x, rows, :] - (half * sound_squared) * div

    def first_layer(x, carry):
        for t in range(YT):
            rows = slice(Y0 + 8 * t, Y0 + 8 * t + 8)
            new = velocity_tile(f0, x, t)
            for k in range(3):
                f1[k, x, rows, :] = new[k]
            f1[3, x, rows, :] = pressure_tile(f0, x, t)
        return carry

    for c in hy1:
        c.wait_recv()
    corners = []
    for d in range(2):
        x = CX - 1 if d == 0 else 0
        for side in range(2):
            for q in range(2):
                i = 2 * side + q
                cs[d, i : i + 1, :] = yr[0, side, q, x : x + 1, :]
        corners.append(
            pltpu.make_async_remote_copy(
                cs.at[d], cr.at[d], css.at[d], crs.at[d],
                device_id=gx_peer(1 if d == 0 else NGX - 1),
            )
        )
        corners[d].start()
    unpack_y(f0, 0, range(4))
    pl.semaphore_wait(known.at[0], 2 + len(ring_peers))
    tell(1, [z_peer(4), z_peer(nz - 4)])
    lax.fori_loop(2, CX, first_layer, 0)
    for c in hx1:
        c.wait_recv()
    unpack_x(f0, 0, range(4))
    first_layer(1, 0)
    first_layer(CX, 0)

    pack_x(f1, 1, (1, 2, 3))
    pack_y(f1, 1, (1, 2, 3))
    hx3 = [x_copy(1, 1, d, 1, 4) for d in range(2)]
    hy3 = [y_copy(1, 1, d, 1, 4) for d in range(2)]
    for c in hx3 + hy3:
        c.start()
    shapes_x[ring] = shapes_t[...]
    shapes_stage = spread(shapes_x, ring, RX, 2, x_peer)

    for c in corners:
        c.wait_recv()
    for d in range(2):
        x, far, sign = (1, 0, 1.0) if d == 0 else (CX, CX + 1, -1.0)
        edge = gx == (0 if d == 0 else NGX - 1)
        for t in range(YT):
            rows, own = slice(Y0 + 8 * t, Y0 + 8 * t + 8), slice(8 * t, 8 * t + 8)
            u, p = f0[0, x, rows, :], f0[3, x, rows, :]
            nu = time_step * xr[0, d, 5, own, :].astype(f32)
            tile = xr[0, d, 4, own, :].astype(f32) + (nu * u + sign * (w_row * u - half * p))
            if t == 0:
                corner = jnp.where(gy == 0, 0.0, cr[d, 1:2, :])
                tile = tile + jnp.where(x8 == 0, nu * corner, 0.0)
            if t == YT - 1:
                corner = jnp.where(gy == NGY - 1, 0.0, cr[d, 3:4, :])
                tile = tile + jnp.where(x8 == 7, nu * corner, 0.0)
            f1[0, far, rows, :] = jnp.where(edge, 0.0, tile)
    for d in range(2):
        sign = 1.0 if d == 0 else -1.0
        edge = gy == (0 if d == 0 else NGY - 1)
        u, p = ys[0, 1 - d, 0], ys[0, 1 - d, 3]
        nu = time_step * yr[0, d, 5]
        low = jnp.where(gx == 0, 0.0, cr[0, 2 * d : 2 * d + 1, :])
        high = jnp.where(gx == NGX - 1, 0.0, cr[1, 2 * d : 2 * d + 1, :])
        tile = yr[0, d, 4] + (nu * u - (sign * half) * p)
        tile = tile + jnp.where(x8 == 0, (nu - w_row) * low, 0.0)
        tile = tile + jnp.where(x8 == CX - 1, (nu + w_row) * high, 0.0)
        yi[d, 0] = jnp.where(edge, 0.0, tile)
        y = Y0 - 1 if d == 0 else Y0 + CY
        for x in range(CX):
            f1[1, x + 1, y : y + 1, :] = yi[d, 0, x : x + 1, :]

    def second_pressure(x, carry):
        for t in range(YT):
            pre_o[x - 1, 8 * t : 8 * t + 8, :] = pressure_tile(f1, x, t)
        return carry

    lax.fori_loop(1, CX + 1, second_pressure, 0)

    for s in range(SL):
        line = cell_s[0, s] >> 8
        layer = line // CY
        samp[s : s + 1, :] = pre_o[layer, pl.ds(line - layer * CY, 1), :]
    sampled = jnp.sum(jnp.where(z_mask, samp[...], 0.0), axis=1, keepdims=True)
    load = (own_area * sampled).astype(bf16).astype(f32)
    g0[plane, 0:1, :] = row_of(load, SL * parity)
    ring_stage.wait_recv()
    g0[plane, 1:2, :] = jnp.sum(ring_b[:, 0:1, :], axis=0)
    pl.semaphore_wait(known.at[1], 2)
    stage0 = spread(g0, plane, nz, 3, z_peer)
    nodes_x[ring] = nodes_t[...]
    nodes_stage = spread(nodes_x, ring, RX, 4, x_peer)
    for c in hx3 + hy3:
        c.wait_recv()
    unpack_x(f1, 1, (1, 2, 3))
    unpack_y(f1, 1, (1, 2, 3))

    def second_velocity(x, carry):
        for t in range(YT):
            new = velocity_tile(f1, x, t)
            for k in range(3):
                vel_o[k, x - 1, 8 * t : 8 * t + 8, :] = new[k]
        return carry

    lax.fori_loop(1, CX + 1, second_velocity, 0)
    for c in hx1 + hy1 + corners + hx3 + hy3 + [ring_stage, damper_stage]:
        c.wait_send()
    damper_stage.wait_recv()

    def table(i, carry):
        low = panels[pl.ds(2 * i + ring // 2, 1), :] & 127
        sub = lax.broadcasted_iota(jnp.int32, (128, 128), 0)
        onehot[:, pl.ds(pl.multiple_of(i * 128, 128), 128)] = (sub == low).astype(f32).astype(bf16)
        return carry

    lax.fori_loop(0, nz, table, 0)

    def paired(buf, row):
        return jnp.concatenate(
            [buf[2 * j, row : row + 1, :] + buf[2 * j + 1, row : row + 1, :] for j in range(NGY // 2)],
            axis=0,
        )

    visc_all, hyst_all, node_all = (paired(dampers_b, r) for r in range(3))
    for j in range(NGY // 2):
        pick_all[:, j * 128 : (j + 1) * 128] = pick(node_all[j : j + 1, :])
    q0_row, v0_row, omega, zeta = (jnp.sum(ring_b[:, r : r + 1, :], axis=0) for r in range(1, 5))

    shapes_stage.wait_recv()
    stage0.wait_recv()
    sub16 = lax.broadcasted_iota(jnp.int32, (16, 128), 0)
    for i in range(nz):
        high = panels[pl.ds(2 * i + ring // 2, 1), :] >> 7
        lhs[:, i * 128 : (i + 1) * 128] = jnp.where(sub16 == high, g0[i, 0:1, :], 0.0).astype(bf16)
    placed = lax.dot_general(
        lhs[...], onehot[...], (((1,), (1,)), ((), ())), preferred_element_type=f32
    )
    parts = []
    for r in range(RX):
        part = jnp.zeros((MB, 128), f32)
        for a in range(16):
            part = part + shapes_x[r, :, a * 128 : (a + 1) * 128].astype(f32) * placed[a : a + 1, :]
        parts.append(row_of(jnp.sum(part, axis=1, keepdims=True), MB * r))

    def response(stretch, rate, viscous, hysteretic, hysteresis):
        hysteresis = hysteresis + modal_step * (
            hysteresis_gain * rate
            - shape_beta * jnp.abs(rate) * hysteresis
            - shape_gamma * rate * jnp.abs(hysteresis)
        )
        return hysteresis, -(viscous * rate + spring_rate * stretch + hysteretic * hysteresis)

    first = jnp.sum(g0[:, 1:2, :], axis=0)
    stretch0 = first[:, 0:DB]
    hysteresis, force = response(stretch0, first[:, DB : 2 * DB], dvisc[...], dhyst[...], dstate[...])
    damper_part = jnp.sum(drift[:, 0:DB] * force, axis=1, keepdims=True)
    spot = ring * NGY + gy
    h1[spot, 0:1, :] = (parts[0] + parts[1]) + (parts[2] + parts[3])
    h1[spot, 1:2, :] = row_of(damper_part, MB * ring)
    h1[spot, 2:3, :] = placed_half(stretch0)
    h1[spot, 3:4, :] = placed_half(hysteresis)

    def plane_peer(k):
        there = lax.rem(spot + k, RX * NGY)
        return {"gx": plane * RX + there // NGY, "gy": lax.rem(there, NGY)}

    stage1 = spread(h1, spot, RX * NGY, 5, plane_peer)
    stage0.wait_send()
    shapes_stage.wait_send()
    nodes_stage.wait_recv()
    drift_x[...] = jnp.dot(
        nodes_x[...].reshape(RX * MB, -1), pick_all[...], preferred_element_type=f32
    )
    nodes_stage.wait_send()
    stage1.wait_recv()
    panel_modal = jnp.sum(h1[:, 0:1, :], axis=0)
    damper_modal = jnp.sum(h1[:, 1:2, :], axis=0)
    stretch_all, hysteresis_all = paired(h1, 2), paired(h1, 3)

    def advance_modes(q, v, damper_load):
        acceleration = (
            panel_modal + damper_load - 2.0 * zeta * omega * v - omega * omega * q
        )
        v = v + modal_step * acceleration
        return q + modal_step * v, v

    q1, v1 = advance_modes(q0_row, v0_row, damper_modal)
    v1_column = column_of(v1, RX * MB)
    for j in range(NGY // 2):
        g2[plane, j : j + 1, :] = jnp.sum(
            drift_x[:, j * 128 : (j + 1) * 128] * v1_column, axis=0, keepdims=True
        )
    stage2 = spread(g2, plane, nz, 6, z_peer)
    stage1.wait_send()
    stage2.wait_recv()
    rate_all = jnp.sum(g2[...], axis=0)
    stretch_all = stretch_all + modal_step * rate_all
    hysteresis_all, force = response(stretch_all, rate_all, visc_all, hyst_all, hysteresis_all)
    late[...] = hysteresis_all
    own = late[pl.ds(gy // 2, 1), :]
    damp_o[...] = jnp.where(odd == 1, own[:, DB : 2 * DB], own[:, 0:DB])
    part = jnp.zeros((MB, 128), f32)
    for j in range(NGY // 2):
        rows = pl.ds(pl.multiple_of(ring * MB, MB), MB)
        part = part + drift_x[rows, j * 128 : (j + 1) * 128] * force[j : j + 1, :]
    damper_modal = row_of(jnp.sum(part, axis=1, keepdims=True), MB * ring)
    q2, v2 = advance_modes(q1, v1, damper_modal)
    modal_o[0:1, :] = row_of(column_of(q2, MB, MB * ring), 0, MB)
    modal_o[1:2, :] = row_of(column_of(v2, MB, MB * ring), 0, MB)
    stage2.wait_send()


def write_out(*refs):
    n = len(refs) // 2
    sem = refs[-1]
    copies = [pltpu.make_async_copy(refs[i], refs[n + i], sem.at[i]) for i in range(n)]
    for c in copies:
        c.start()
    for c in copies:
        c.wait()


def body(
    velocity, pressure, viscosity, wind_profile, panel_area, slot_cell, slot_panel, panel_shapes,
    node_shapes, damper_node, damper_viscous, damper_hysteretic, frequency, damping_ratio,
    modal_state, damper_state,
):
    hbm = pl.BlockSpec(memory_space=pltpu.MemorySpace.HBM)
    vmem = pl.BlockSpec(memory_space=pltpu.VMEM)
    f32, bf16 = jnp.float32, jnp.bfloat16
    slots = slot_panel.shape[1]
    small = (
        wind_profile.reshape(1, -1), panel_area.reshape(1, -1),
        slot_cell, slot_cell, slot_panel.reshape(slots // 128, 128), panel_shapes.T, node_shapes.T,
        damper_node.reshape(1, -1), damper_viscous.reshape(1, -1), damper_hysteretic.reshape(1, -1),
        frequency.reshape(1, -1), damping_ratio.reshape(1, -1), modal_state,
        damper_state.reshape(1, -1),
    )
    outs = (
        jax.ShapeDtypeStruct(velocity.shape, f32),
        jax.ShapeDtypeStruct(pressure.shape, f32),
        jax.ShapeDtypeStruct(modal_state.shape, f32),
        jax.ShapeDtypeStruct((1, DB), f32),
    )
    held = [
        (pltpu.SMEM if i == 2 else pltpu.VMEM)(a.shape, a.dtype) for i, a in enumerate(small)
    ]
    results = pl.pallas_call(
        kernel,
        out_shape=outs,
        in_specs=[hbm] * (3 + len(small)),
        out_specs=(vmem,) * 4,
        scratch_shapes=held + [
            pltpu.VMEM((4, CX + 2, CY + 16, NZ), f32),
            pltpu.VMEM((4, CX + 2, CY + 16, NZ), f32),
            pltpu.VMEM((CX, CY, NZ), f32),
            pltpu.VMEM((2, 2, 6, CY, NZ), bf16),
            pltpu.VMEM((2, 2, 6, CY, NZ), bf16),
            pltpu.VMEM((2, 2, 6, CX, NZ), f32),
            pltpu.VMEM((2, 2, 6, CX, NZ), f32),
            pltpu.VMEM((2, 2, CX, NZ), f32),
            pltpu.VMEM((2, 4, NZ), f32),
            pltpu.VMEM((2, 4, NZ), f32),
            pltpu.VMEM((SL, NZ), f32),
            pltpu.VMEM((128, NGX // RX * 128), bf16),
            pltpu.VMEM((16, NGX // RX * 128), bf16),
            pltpu.VMEM((RX,) + panel_shapes.shape[::-1], bf16),
            pltpu.VMEM((RX,) + node_shapes.shape[::-1], bf16),
            pltpu.VMEM((node_shapes.shape[0], DB * NGY), bf16),
            pltpu.VMEM((RX * MB, DB * NGY), f32),
            pltpu.VMEM((RX, 8, 128), f32),
            pltpu.VMEM((NGY, 4, 128), f32),
            pltpu.VMEM((NGX // RX, 2, 128), f32),
            pltpu.VMEM((RX * NGY, 4, 128), f32),
            pltpu.VMEM((NGX // RX, NGY // 2, 128), f32),
            pltpu.VMEM((NGY // 2, 128), f32),
            pltpu.SemaphoreType.DMA((3,)),
            pltpu.SemaphoreType.DMA((len(small),)),
            pltpu.SemaphoreType.DMA((2, 4)),
            pltpu.SemaphoreType.DMA((2, 4)),
            pltpu.SemaphoreType.DMA((2, 4)),
            pltpu.SemaphoreType.DMA((2, 4)),
            pltpu.SemaphoreType.DMA((2,)),
            pltpu.SemaphoreType.DMA((2,)),
            pltpu.SemaphoreType.DMA((7,)),
            pltpu.SemaphoreType.DMA((7,)),
            pltpu.SemaphoreType.REGULAR((2,)),
        ],
        compiler_params=pltpu.CompilerParams(
            collective_id=0, has_side_effects=True, vmem_limit_bytes=40 << 20
        ),
    )(*[pltpu.with_memory_space_constraint(a, pltpu.MemorySpace.HBM) for a in (velocity, pressure, viscosity, *small)])
    vel, pre, modal, damp = pl.pallas_call(
        write_out,
        out_shape=outs,
        in_specs=[vmem] * 4,
        out_specs=(hbm,) * 4,
        scratch_shapes=[pltpu.SemaphoreType.DMA((4,))], compiler_params=pltpu.CompilerParams(vmem_limit_bytes=1 << 20),
    )(*results)
    return vel, pre, modal, damp.reshape(-1)


def solution(mesh):
    placed = (
        P(None, "gx", "gy", None),
        P("gx", "gy", None),
        P("gx", "gy", None),
        P(),
        P("gy"),
        P("gy", "gx"),
        P("gy", None),
        P("gy", "gx"),
        P(None, "gx"),
        P("gy"),
        P("gy"),
        P("gy"),
        P("gx"),
        P("gx"),
        P(None, "gx"),
        P("gy"),
    )
    return jax.shard_map(
        body,
        mesh=mesh,
        in_specs=placed,
        out_specs=(P(None, "gx", "gy", None), P("gx", "gy", None), P(None, "gx"), P("gy")),
        check_vma=False,
    )
```

```python
import jax
import jax.numpy as jnp
from jax import lax
from jax.experimental import pallas as pl
from jax.experimental.pallas import tpu as pltpu
from jax.sharding import PartitionSpec as P

time_step = 0.1
sound_squared = 1.0
modal_step = 0.5
hysteresis_gain = 1.0
shape_beta = 0.5
shape_gamma = 0.5
spring_rate = 0.5

CX, CY, NZ = 8, 48, 256
NGX, NGY = 64, 8
RX = 4
MB = 32
DB = 64
SL = 64
Y0 = 8
YT = CY // 8


def row_of(column, lane_shift=0, lanes=128):
    n = column.shape[0]
    sub = lax.broadcasted_iota(jnp.int32, (n, lanes), 0)
    lane = lax.broadcasted_iota(jnp.int32, (n, lanes), 1)
    return jnp.sum(jnp.where(lane == sub + lane_shift, column, 0.0), axis=0, keepdims=True)


def column_of(row, n, lane_shift=0):
    lanes = row.shape[1]
    sub = lax.broadcasted_iota(jnp.int32, (n, lanes), 0)
    lane = lax.broadcasted_iota(jnp.int32, (n, lanes), 1)
    zero = jnp.zeros((), row.dtype)
    return jnp.sum(jnp.where(lane == sub + lane_shift, row, zero), axis=1, keepdims=True)


def twice(row):
    return jnp.concatenate([row, row], axis=1)


def kernel(
    vel_h, pre_h, vis_h, *refs,
):
    small_h = refs[:14]
    (
        vel_o, pre_o, modal_o, damp_o,
        wind, area, cell_s, cell_v, panels, shapes_t, nodes_t,
        dnode, dvisc, dhyst, freq, ratio, modal, dstate,
        f0, f1, vis, xs, xr, ys, yr, yi, cs, cr, samp, onehot, lhs,
        shapes_x, nodes_x, pick_all, drift_x, ring_b, dampers_b, g0, h1, g2, late,
        in_sem, small_sem, xss, xrs, yss, yrs, css, crs, s_sem, r_sem, known,
    ) = refs[14:]
    gx = lax.axis_index("gx")
    gy = lax.axis_index("gy")
    f32, bf16 = jnp.float32, jnp.bfloat16

    def gx_peer(k):
        return {"gx": lax.rem(gx + k, NGX)}

    def gy_peer(k):
        return {"gy": lax.rem(gy + k, NGY)}

    barrier = pltpu.get_barrier_semaphore()

    plane, ring = gx // RX, lax.rem(gx, RX)

    def z_peer(k):
        return {"gx": lax.rem(plane + k, NGX // RX) * RX + ring}

    def x_peer(k):
        return {"gx": plane * RX + lax.rem(ring + k, RX)}

    nz = NGX // RX
    near = [gx_peer(1), gx_peer(NGX - 1)]
    near += [z_peer(k) for k in (1, nz - 1, 2, nz - 2)]
    near += [x_peer(k) for k in range(1, RX)]
    near += [gy_peer(k) for k in range(1, NGY)]
    ring_peers = [x_peer(k) for k in range(1, RX)]
    for peer in near:
        pl.semaphore_signal(barrier, 1, device_id=peer)

    def tell(i, peers):
        for peer in peers:
            pl.semaphore_signal(known.at[i], 1, device_id=peer)

    cv = pltpu.make_async_copy(vel_h, f0.at[0:3, 1 : 1 + CX, Y0 : Y0 + CY, :], in_sem.at[0])
    cp = pltpu.make_async_copy(pre_h, f0.at[3, 1 : 1 + CX, Y0 : Y0 + CY, :], in_sem.at[1])
    cn = pltpu.make_async_copy(vis_h, vis, in_sem.at[2])
    cv.start()
    cp.start()
    cn.start()
    small = [
        pltpu.make_async_copy(src, dst, small_sem.at[i])
        for i, (src, dst) in enumerate(
            zip(
                small_h,
                (wind, area, cell_s, cell_v, panels, shapes_t, nodes_t,
                 dnode, dvisc, dhyst, freq, ratio, modal, dstate),
            )
        )
    ]
    for c in small:
        c.start()
    cv.wait()
    cp.wait()

    y_order = (1, 0, 2, 3)

    def pack_x(f, p, comps):
        for k in comps:
            xs[p, 0, k] = f[k, CX, Y0 : Y0 + CY, :].astype(bf16)
            xs[p, 1, k] = f[k, 1, Y0 : Y0 + CY, :].astype(bf16)

    def pack_y(f, p, slots):
        for q in slots:
            k = y_order[q]
            for x in range(CX):
                ys[p, 0, q, x : x + 1, :] = f[k, x + 1, Y0 + CY - 1 : Y0 + CY, :]
                ys[p, 1, q, x : x + 1, :] = f[k, x + 1, Y0 : Y0 + 1, :]

    def x_copy(p, part, d, lo, hi):
        i = 2 * part + d
        return pltpu.make_async_remote_copy(
            xs.at[p, d, lo:hi], xr.at[p, d, lo:hi], xss.at[p, i], xrs.at[p, i],
            device_id=gx_peer(1 if d == 0 else NGX - 1),
        )

    def y_copy(p, part, d, lo, hi):
        i = 2 * part + d
        return pltpu.make_async_remote_copy(
            ys.at[p, d, lo:hi], yr.at[p, d, lo:hi], yss.at[p, i], yrs.at[p, i],
            device_id=gy_peer(1 if d == 0 else NGY - 1),
        )

    def unpack_x(f, p, comps):
        for k in comps:
            f[k, 0, Y0 : Y0 + CY, :] = jnp.where(gx == 0, 0.0, xr[p, 0, k].astype(f32))
            f[k, CX + 1, Y0 : Y0 + CY, :] = jnp.where(gx == NGX - 1, 0.0, xr[p, 1, k].astype(f32))

    def unpack_y(f, p, slots):
        for q in slots:
            k = y_order[q]
            for x in range(CX):
                f[k, x + 1, Y0 - 1 : Y0, :] = jnp.where(gy == 0, 0.0, yr[p, 0, q, x : x + 1, :])
                f[k, x + 1, Y0 + CY : Y0 + CY + 1, :] = jnp.where(
                    gy == NGY - 1, 0.0, yr[p, 1, q, x : x + 1, :]
                )

    lane8 = lax.broadcasted_iota(jnp.int32, (8, NZ), 1)

    def above(v):
        return jnp.where(lane8 == NZ - 1, 0.0, pltpu.roll(v, NZ - 1, 1))

    def below(v):
        return jnp.where(lane8 == 0, 0.0, pltpu.roll(v, 1, 1))

    small[0].wait()
    w_row = jnp.broadcast_to((-0.5 * time_step) * wind[...], (8, NZ))
    half = 0.5 * time_step

    x8 = lax.broadcasted_iota(jnp.int32, (CX, NZ), 0)

    def next_x(v):
        return jnp.where(x8 == CX - 1, 0.0, pltpu.roll(v, CX - 1, 0))

    def last_x(v):
        return jnp.where(x8 == 0, 0.0, pltpu.roll(v, 1, 0))

    def outer_x(d):
        x, inner, sign = (CX, CX - 1, 1.0) if d == 0 else (1, 2, -1.0)
        zero = jnp.zeros((1, NZ), f32)
        f0[0, x, Y0 - 1 : Y0, :] = zero
        f0[0, x, Y0 + CY : Y0 + CY + 1, :] = zero
        for t in range(YT):
            rows = pl.ds(Y0 + 8 * t, 8)
            own = slice(8 * t, 8 * t + 8)
            c, i, p = f0[0, x, rows, :], f0[0, inner, rows, :], f0[3, inner, rows, :]
            r, l = f0[0, x, pl.ds(Y0 + 8 * t + 1, 8), :], f0[0, x, pl.ds(Y0 + 8 * t - 1, 8), :]
            lap = (i + (r + l)) + ((above(c) + below(c)) - 6.0 * c)
            nu = time_step * vis[x - 1, own, :]
            tile = c + (nu * lap + sign * (half * p - w_row * i))
            yield own, tile, vis[x - 1, own, :]

    def pack_outer_x():
        for d in range(2):
            for own, tile, nu in outer_x(d):
                xs[0, d, 4, own, :] = tile.astype(bf16)
                xs[0, d, 5, own, :] = nu.astype(bf16)

    def pack_outer_y():
        for d in range(2):
            y, inner, sign = (Y0 + CY - 1, Y0 + CY - 2, 1.0) if d == 0 else (Y0, Y0 + 1, -1.0)
            for x in range(CX):
                yi[d, 0, x : x + 1, :] = f0[1, x + 1, inner : inner + 1, :]
                yi[d, 1, x : x + 1, :] = f0[3, x + 1, inner : inner + 1, :]
                ys[0, d, 5, x : x + 1, :] = vis[x, y - Y0 : y - Y0 + 1, :]
            c, nu = ys[0, d, 0], time_step * ys[0, d, 5]
            a, b = next_x(c), last_x(c)
            lap = (yi[d, 0] + (a + b)) + ((above(c) + below(c)) - 6.0 * c)
            ys[0, d, 4] = c + (w_row * (a - b) + nu * lap + (sign * half) * yi[d, 1])

    pack_y(f0, 0, range(4))
    cn.wait()
    pack_outer_y()
    pack_x(f0, 0, range(4))
    pack_outer_x()
    pl.semaphore_wait(barrier, len(near))
    tell(0, [z_peer(2), z_peer(nz - 2)] + ring_peers)
    hx1 = [x_copy(0, 0, d, 0, 6) for d in range(2)]
    hy1 = [y_copy(0, 0, d, 0, 6) for d in range(2)]
    for c in hy1 + hx1:
        c.start()

    for c in small[1:]:
        c.wait()
    dn = dnode[...].astype(f32)
    dn2 = twice(dn)
    node_no = lax.broadcasted_iota(jnp.int32, (nodes_t.shape[1], 2 * DB), 0).astype(f32)

    def pick(row):
        return jnp.where(node_no == row + 1.0, 1.0, jnp.where(node_no == row, -1.0, 0.0)).astype(bf16)

    drift = jnp.dot(nodes_t[...], pick(dn2), preferred_element_type=f32)
    q0 = column_of(modal[0:1, :], MB)
    v0 = column_of(modal[1:2, :], MB)
    first_half = lax.broadcasted_iota(jnp.int32, (MB, 2 * DB), 1) < DB
    odd = lax.rem(gy, 2)
    own_half = (lax.broadcasted_iota(jnp.int32, (1, 2 * DB), 1) // DB) == odd

    def placed_half(row):
        return jnp.where(own_half, twice(row), 0.0)

    dampers_b[gy, 0:1, :] = placed_half(dvisc[...])
    dampers_b[gy, 1:2, :] = placed_half(dhyst[...])
    dampers_b[gy, 2:3, :] = placed_half(dn)
    ring_b[ring, 0:1, :] = jnp.sum(
        drift * jnp.where(first_half, q0, v0), axis=0, keepdims=True
    )
    ring_b[ring, 1:2, :] = row_of(q0, MB * ring)
    ring_b[ring, 2:3, :] = row_of(v0, MB * ring)
    ring_b[ring, 3:4, :] = row_of(column_of(freq[...], MB), MB * ring)
    ring_b[ring, 4:5, :] = row_of(column_of(ratio[...], MB), MB * ring)

    def spread(buf, me, peers, sem_no):
        for peer in peers:
            pltpu.make_async_remote_copy(
                buf.at[me], buf.at[me], s_sem.at[sem_no], r_sem.at[sem_no], device_id=peer
            ).start()
        most = buf.at[pl.ds(0, len(peers))]
        return pltpu.make_async_remote_copy(
            most, most, s_sem.at[sem_no], r_sem.at[sem_no], device_id=peers[0]
        )

    def far_first(n):
        return sorted(range(n), key=lambda k: -min(k, n - k))

    z_peers = [z_peer(k) for k in far_first(nz)[:-1]]
    gy_peers = [gy_peer(k) for k in far_first(NGY)[:-1]]
    x_peers = [x_peer(k) for k in far_first(RX)[:-1]]

    ring_stage = spread(ring_b, ring, x_peers, 0)
    damper_stage = spread(dampers_b, gy, gy_peers, 1)

    parity = lax.rem(gx, 2)
    own_ids = column_of(panels[pl.ds(gx // 2, 1), :], SL, SL * parity)
    panel_no = lax.broadcasted_iota(jnp.int32, (SL, area.shape[1]), 1)
    own_area = jnp.sum(jnp.where(panel_no == own_ids, area[...], 0.0), axis=1, keepdims=True)
    own_z = column_of(cell_v[...], SL) & (NZ - 1)
    z_mask = (lax.broadcasted_iota(jnp.int32, (SL, NZ), 1) == own_z)

    def velocity_tile(f, x, t):
        rows = pl.ds(Y0 + 8 * t, 8)
        rows_m = pl.ds(Y0 + 8 * t - 1, 8)
        rows_p = pl.ds(Y0 + 8 * t + 1, 8)
        nu = time_step * vis[x - 1, 8 * t : 8 * t + 8, :]
        pc = f[3, x, rows, :]
        slope = (
            f[3, x + 1, rows, :] - f[3, x - 1, rows, :],
            f[3, x, rows_p, :] - f[3, x, rows_m, :],
            above(pc) - below(pc),
        )
        out = []
        for k in range(3):
            c = f[k, x, rows, :]
            a, b = f[k, x + 1, rows, :], f[k, x - 1, rows, :]
            r, l = f[k, x, rows_p, :], f[k, x, rows_m, :]
            u, d = above(c), below(c)
            lap = ((a + b) + (r + l)) + ((u + d) - 6.0 * c)
            out.append(c + (w_row * (a - b) + nu * lap - half * slope[k]))
        return out

    def pressure_tile(f, x, t):
        rows = pl.ds(Y0 + 8 * t, 8)
        rows_m = pl.ds(Y0 + 8 * t - 1, 8)
        rows_p = pl.ds(Y0 + 8 * t + 1, 8)
        w = f[2, x, rows, :]
        div = (f[0, x + 1, rows, :] - f[0, x - 1, rows, :]) + (
            (f[1, x, rows_p, :] - f[1, x, rows_m, :]) + (above(w) - below(w))
        )
        return f[3, x, rows, :] - (half * sound_squared) * div

    def first_layer(x, carry):
        for t in range(YT):
            rows = slice(Y0 + 8 * t, Y0 + 8 * t + 8)
            new = velocity_tile(f0, x, t)
            for k in range(3):
                f1[k, x, rows, :] = new[k]
            f1[3, x, rows, :] = pressure_tile(f0, x, t)
        return carry

    shapes_x[ring] = shapes_t[...]
    nodes_x[ring] = nodes_t[...]
    for c in hy1:
        c.wait_recv()
    corners = []
    for d in range(2):
        x = CX - 1 if d == 0 else 0
        for side in range(2):
            for q in range(2):
                i = 2 * side + q
                cs[d, i : i + 1, :] = yr[0, side, q, x : x + 1, :]
        corners.append(
            pltpu.make_async_remote_copy(
                cs.at[d], cr.at[d], css.at[d], crs.at[d],
                device_id=gx_peer(1 if d == 0 else NGX - 1),
            )
        )
        corners[d].start()
    unpack_y(f0, 0, range(4))
    pl.semaphore_wait(known.at[0], 2 + len(ring_peers))
    tell(1, [z_peer(4), z_peer(nz - 4)])
    lax.fori_loop(2, CX, first_layer, 0)
    for c in hx1:
        c.wait_recv()
    shapes_stage = spread(shapes_x, ring, x_peers, 2)
    unpack_x(f0, 0, range(4))
    first_layer(1, 0)
    first_layer(CX, 0)


    for c in corners:
        c.wait_recv()
    for d in range(2):
        x, far, sign = (1, 0, 1.0) if d == 0 else (CX, CX + 1, -1.0)
        edge = gx == (0 if d == 0 else NGX - 1)
        for t in range(YT):
            rows, own = slice(Y0 + 8 * t, Y0 + 8 * t + 8), slice(8 * t, 8 * t + 8)
            u, p = f0[0, x, rows, :], f0[3, x, rows, :]
            nu = time_step * xr[0, d, 5, own, :].astype(f32)
            tile = xr[0, d, 4, own, :].astype(f32) + (nu * u + sign * (w_row * u - half * p))
            if t == 0:
                corner = jnp.where(gy == 0, 0.0, cr[d, 1:2, :])
                tile = tile + jnp.where(x8 == 0, nu * corner, 0.0)
            if t == YT - 1:
                corner = jnp.where(gy == NGY - 1, 0.0, cr[d, 3:4, :])
                tile = tile + jnp.where(x8 == 7, nu * corner, 0.0)
            f1[0, far, rows, :] = jnp.where(edge, 0.0, tile)
    for d in range(2):
        sign = 1.0 if d == 0 else -1.0
        edge = gy == (0 if d == 0 else NGY - 1)
        u, p = ys[0, 1 - d, 0], ys[0, 1 - d, 3]
        nu = time_step * yr[0, d, 5]
        low = jnp.where(gx == 0, 0.0, cr[0, 2 * d : 2 * d + 1, :])
        high = jnp.where(gx == NGX - 1, 0.0, cr[1, 2 * d : 2 * d + 1, :])
        tile = yr[0, d, 4] + (nu * u - (sign * half) * p)
        tile = tile + jnp.where(x8 == 0, (nu - w_row) * low, 0.0)
        tile = tile + jnp.where(x8 == CX - 1, (nu + w_row) * high, 0.0)
        yi[d, 0] = jnp.where(edge, 0.0, tile)
        y = Y0 - 1 if d == 0 else Y0 + CY
        for x in range(CX):
            f1[1, x + 1, y : y + 1, :] = yi[d, 0, x : x + 1, :]

    def second_pressure(x, carry):
        for t in range(YT):
            pre_o[x - 1, 8 * t : 8 * t + 8, :] = pressure_tile(f1, x, t)
        return carry

    lax.fori_loop(1, CX + 1, second_pressure, 0)

    for s in range(SL):
        line = cell_s[0, s] >> 8
        layer = line // CY
        samp[s : s + 1, :] = pre_o[layer, pl.ds(line - layer * CY, 1), :]
    sampled = jnp.sum(jnp.where(z_mask, samp[...], 0.0), axis=1, keepdims=True)
    load = (own_area * sampled).astype(bf16).astype(f32)
    g0[plane, 0:1, :] = row_of(load, SL * parity)
    ring_stage.wait_recv()
    g0[plane, 1:2, :] = jnp.sum(ring_b[:, 0:1, :], axis=0)
    pl.semaphore_wait(known.at[1], 2)
    stage0 = spread(g0, plane, z_peers, 3)
    nodes_stage = spread(nodes_x, ring, x_peers, 4)
    pack_x(f1, 1, (1, 2, 3))
    pack_y(f1, 1, (1, 2, 3))
    hx3 = [x_copy(1, 1, d, 1, 4) for d in range(2)]
    hy3 = [y_copy(1, 1, d, 1, 4) for d in range(2)]
    for c in hx3 + hy3:
        c.start()
    for c in hx1 + hy1 + corners + [ring_stage, damper_stage]:
        c.wait_send()
    damper_stage.wait_recv()

    def table(i, carry):
        low = panels[pl.ds(2 * i + ring // 2, 1), :] & 127
        sub = lax.broadcasted_iota(jnp.int32, (128, 128), 0)
        onehot[:, pl.ds(pl.multiple_of(i * 128, 128), 128)] = (sub == low).astype(f32).astype(bf16)
        return carry

    lax.fori_loop(0, nz, table, 0)

    def paired(buf, row):
        return jnp.concatenate(
            [buf[2 * j, row : row + 1, :] + buf[2 * j + 1, row : row + 1, :] for j in range(NGY // 2)],
            axis=0,
        )

    visc_all, hyst_all, node_all = (paired(dampers_b, r) for r in range(3))
    for j in range(NGY // 2):
        pick_all[:, j * 128 : (j + 1) * 128] = pick(node_all[j : j + 1, :])
    q0_row, v0_row, omega, zeta = (jnp.sum(ring_b[:, r : r + 1, :], axis=0) for r in range(1, 5))

    shapes_stage.wait_recv()
    stage0.wait_recv()
    sub16 = lax.broadcasted_iota(jnp.int32, (16, 128), 0)
    for i in range(nz):
        high = panels[pl.ds(2 * i + ring // 2, 1), :] >> 7
        lhs[:, i * 128 : (i + 1) * 128] = jnp.where(sub16 == high, g0[i, 0:1, :], 0.0).astype(bf16)
    placed = lax.dot_general(
        lhs[...], onehot[...], (((1,), (1,)), ((), ())), preferred_element_type=f32
    )
    parts = []
    for r in range(RX):
        part = jnp.zeros((MB, 128), f32)
        for a in range(16):
            part = part + shapes_x[r, :, a * 128 : (a + 1) * 128].astype(f32) * placed[a : a + 1, :]
        parts.append(row_of(jnp.sum(part, axis=1, keepdims=True), MB * r))

    def response(stretch, rate, viscous, hysteretic, hysteresis):
        hysteresis = hysteresis + modal_step * (
            hysteresis_gain * rate
            - shape_beta * jnp.abs(rate) * hysteresis
            - shape_gamma * rate * jnp.abs(hysteresis)
        )
        return hysteresis, -(viscous * rate + spring_rate * stretch + hysteretic * hysteresis)

    first = jnp.sum(g0[:, 1:2, :], axis=0)
    stretch0 = first[:, 0:DB]
    hysteresis, force = response(stretch0, first[:, DB : 2 * DB], dvisc[...], dhyst[...], dstate[...])
    damper_part = jnp.sum(drift[:, 0:DB] * force, axis=1, keepdims=True)
    spot = ring * NGY + gy
    h1[spot, 0:1, :] = (parts[0] + parts[1]) + (parts[2] + parts[3])
    h1[spot, 1:2, :] = row_of(damper_part, MB * ring)
    h1[spot, 2:3, :] = placed_half(stretch0)
    h1[spot, 3:4, :] = placed_half(hysteresis)

    plane_peers = []
    steps = [(a, b, c) for a in range(RX) for b in range(NGY // 2) for c in range(2)]
    for a, b, c in sorted(steps, key=lambda k: -min(k[0], RX - k[0]) - min(k[1], NGY // 2 - k[1])):
        if a or b or c:
            there = 2 * lax.rem(gy // 2 + b, NGY // 2) + lax.rem(odd + c, 2)
            plane_peers.append({"gx": plane * RX + lax.rem(ring + a, RX), "gy": there})
    stage1 = spread(h1, spot, plane_peers, 5)
    stage0.wait_send()
    shapes_stage.wait_send()
    nodes_stage.wait_recv()
    drift_x[...] = jnp.dot(
        nodes_x[...].reshape(RX * MB, -1), pick_all[...], preferred_element_type=f32
    )
    nodes_stage.wait_send()
    stage1.wait_recv()
    panel_modal = jnp.sum(h1[:, 0:1, :], axis=0)
    damper_modal = jnp.sum(h1[:, 1:2, :], axis=0)
    stretch_all, hysteresis_all = paired(h1, 2), paired(h1, 3)

    def advance_modes(q, v, damper_load):
        acceleration = (
            panel_modal + damper_load - 2.0 * zeta * omega * v - omega * omega * q
        )
        v = v + modal_step * acceleration
        return q + modal_step * v, v

    q1, v1 = advance_modes(q0_row, v0_row, damper_modal)
    v1_column = column_of(v1, RX * MB)
    for j in range(NGY // 2):
        g2[plane, j : j + 1, :] = jnp.sum(
            drift_x[:, j * 128 : (j + 1) * 128] * v1_column, axis=0, keepdims=True
        )
    stage2 = spread(g2, plane, z_peers, 6)
    stage1.wait_send()
    for c in hx3 + hy3:
        c.wait_recv()
    unpack_x(f1, 1, (1, 2, 3))
    unpack_y(f1, 1, (1, 2, 3))

    def second_velocity(x, carry):
        for t in range(YT):
            new = velocity_tile(f1, x, t)
            for k in range(3):
                vel_o[k, x - 1, 8 * t : 8 * t + 8, :] = new[k]
        return carry

    lax.fori_loop(1, CX + 1, second_velocity, 0)
    for c in hx3 + hy3:
        c.wait_send()
    stage2.wait_recv()
    rate_all = jnp.sum(g2[...], axis=0)
    stretch_all = stretch_all + modal_step * rate_all
    hysteresis_all, force = response(stretch_all, rate_all, visc_all, hyst_all, hysteresis_all)
    late[...] = hysteresis_all
    own = late[pl.ds(gy // 2, 1), :]
    damp_o[...] = jnp.where(odd == 1, own[:, DB : 2 * DB], own[:, 0:DB])
    part = jnp.zeros((MB, 128), f32)
    for j in range(NGY // 2):
        rows = pl.ds(pl.multiple_of(ring * MB, MB), MB)
        part = part + drift_x[rows, j * 128 : (j + 1) * 128] * force[j : j + 1, :]
    damper_modal = row_of(jnp.sum(part, axis=1, keepdims=True), MB * ring)
    q2, v2 = advance_modes(q1, v1, damper_modal)
    modal_o[0:1, :] = row_of(column_of(q2, MB, MB * ring), 0, MB)
    modal_o[1:2, :] = row_of(column_of(v2, MB, MB * ring), 0, MB)
    stage2.wait_send()


def write_out(*refs):
    n = len(refs) // 2
    sem = refs[-1]
    copies = [pltpu.make_async_copy(refs[i], refs[n + i], sem.at[i]) for i in range(n)]
    for c in copies:
        c.start()
    for c in copies:
        c.wait()


def body(
    velocity, pressure, viscosity, wind_profile, panel_area, slot_cell, slot_panel, panel_shapes,
    node_shapes, damper_node, damper_viscous, damper_hysteretic, frequency, damping_ratio,
    modal_state, damper_state,
):
    hbm = pl.BlockSpec(memory_space=pltpu.MemorySpace.HBM)
    vmem = pl.BlockSpec(memory_space=pltpu.VMEM)
    f32, bf16 = jnp.float32, jnp.bfloat16
    slots = slot_panel.shape[1]
    small = (
        wind_profile.reshape(1, -1), panel_area.reshape(1, -1),
        slot_cell, slot_cell, slot_panel.reshape(slots // 128, 128), panel_shapes.T, node_shapes.T,
        damper_node.reshape(1, -1), damper_viscous.reshape(1, -1), damper_hysteretic.reshape(1, -1),
        frequency.reshape(1, -1), damping_ratio.reshape(1, -1), modal_state,
        damper_state.reshape(1, -1),
    )
    outs = (
        jax.ShapeDtypeStruct(velocity.shape, f32),
        jax.ShapeDtypeStruct(pressure.shape, f32),
        jax.ShapeDtypeStruct(modal_state.shape, f32),
        jax.ShapeDtypeStruct((1, DB), f32),
    )
    held = [
        (pltpu.SMEM if i == 2 else pltpu.VMEM)(a.shape, a.dtype) for i, a in enumerate(small)
    ]
    results = pl.pallas_call(
        kernel,
        out_shape=outs,
        in_specs=[hbm] * (3 + len(small)),
        out_specs=(vmem,) * 4,
        scratch_shapes=held + [
            pltpu.VMEM((4, CX + 2, CY + 16, NZ), f32),
            pltpu.VMEM((4, CX + 2, CY + 16, NZ), f32),
            pltpu.VMEM((CX, CY, NZ), f32),
            pltpu.VMEM((2, 2, 6, CY, NZ), bf16),
            pltpu.VMEM((2, 2, 6, CY, NZ), bf16),
            pltpu.VMEM((2, 2, 6, CX, NZ), f32),
            pltpu.VMEM((2, 2, 6, CX, NZ), f32),
            pltpu.VMEM((2, 2, CX, NZ), f32),
            pltpu.VMEM((2, 4, NZ), f32),
            pltpu.VMEM((2, 4, NZ), f32),
            pltpu.VMEM((SL, NZ), f32),
            pltpu.VMEM((128, NGX // RX * 128), bf16),
            pltpu.VMEM((16, NGX // RX * 128), bf16),
            pltpu.VMEM((RX,) + panel_shapes.shape[::-1], bf16),
            pltpu.VMEM((RX,) + node_shapes.shape[::-1], bf16),
            pltpu.VMEM((node_shapes.shape[0], DB * NGY), bf16),
            pltpu.VMEM((RX * MB, DB * NGY), f32),
            pltpu.VMEM((RX, 8, 128), f32),
            pltpu.VMEM((NGY, 4, 128), f32),
            pltpu.VMEM((NGX // RX, 2, 128), f32),
            pltpu.VMEM((RX * NGY, 4, 128), f32),
            pltpu.VMEM((NGX // RX, NGY // 2, 128), f32),
            pltpu.VMEM((NGY // 2, 128), f32),
            pltpu.SemaphoreType.DMA((3,)),
            pltpu.SemaphoreType.DMA((len(small),)),
            pltpu.SemaphoreType.DMA((2, 4)),
            pltpu.SemaphoreType.DMA((2, 4)),
            pltpu.SemaphoreType.DMA((2, 4)),
            pltpu.SemaphoreType.DMA((2, 4)),
            pltpu.SemaphoreType.DMA((2,)),
            pltpu.SemaphoreType.DMA((2,)),
            pltpu.SemaphoreType.DMA((7,)),
            pltpu.SemaphoreType.DMA((7,)),
            pltpu.SemaphoreType.REGULAR((2,)),
        ],
        compiler_params=pltpu.CompilerParams(
            collective_id=0, has_side_effects=True, vmem_limit_bytes=40 << 20
        ),
    )(*[pltpu.with_memory_space_constraint(a, pltpu.MemorySpace.HBM) for a in (velocity, pressure, viscosity, *small)])
    vel, pre, modal, damp = pl.pallas_call(
        write_out,
        out_shape=outs,
        in_specs=[vmem] * 4,
        out_specs=(hbm,) * 4,
        scratch_shapes=[pltpu.SemaphoreType.DMA((4,))], compiler_params=pltpu.CompilerParams(vmem_limit_bytes=1 << 20),
    )(*results)
    return vel, pre, modal, damp.reshape(-1)


def solution(mesh):
    placed = (
        P(None, "gx", "gy", None),
        P("gx", "gy", None),
        P("gx", "gy", None),
        P(),
        P("gy"),
        P("gy", "gx"),
        P("gy", None),
        P("gy", "gx"),
        P(None, "gx"),
        P("gy"),
        P("gy"),
        P("gy"),
        P("gx"),
        P("gx"),
        P(None, "gx"),
        P("gy"),
    )
    return jax.shard_map(
        body,
        mesh=mesh,
        in_specs=placed,
        out_specs=(P(None, "gx", "gy", None), P("gx", "gy", None), P(None, "gx"), P("gy")),
        check_vma=False,
    )
```

```python
import jax
import jax.numpy as jnp
from jax import lax
from jax.experimental import pallas as pl
from jax.experimental.pallas import tpu as pltpu
from jax.sharding import PartitionSpec as P

time_step = 0.1
sound_squared = 1.0
modal_step = 0.5
hysteresis_gain = 1.0
shape_beta = 0.5
shape_gamma = 0.5
spring_rate = 0.5

CX, CY, NZ = 8, 48, 256
NGX, NGY = 64, 8
RX = 4
MB = 32
DB = 64
SL = 64
Y0 = 8
YT = CY // 8


def row_of(column, lane_shift=0, lanes=128):
    n = column.shape[0]
    sub = lax.broadcasted_iota(jnp.int32, (n, lanes), 0)
    lane = lax.broadcasted_iota(jnp.int32, (n, lanes), 1)
    return jnp.sum(jnp.where(lane == sub + lane_shift, column, 0.0), axis=0, keepdims=True)


def column_of(row, n, lane_shift=0):
    lanes = row.shape[1]
    sub = lax.broadcasted_iota(jnp.int32, (n, lanes), 0)
    lane = lax.broadcasted_iota(jnp.int32, (n, lanes), 1)
    zero = jnp.zeros((), row.dtype)
    return jnp.sum(jnp.where(lane == sub + lane_shift, row, zero), axis=1, keepdims=True)


def twice(row):
    return jnp.concatenate([row, row], axis=1)


def kernel(
    vel_h, pre_h, vis_h, *refs,
):
    small_h = refs[:14]
    (
        vel_o, pre_o, modal_o, damp_o,
        wind, area, cell_s, cell_v, panels, shapes_t, nodes_t,
        dnode, dvisc, dhyst, freq, ratio, modal, dstate,
        f0, f1, vis, xs, xr, ys, yr, yi, cs, cr, samp, onehot, lhs,
        shapes_x, nodes_x, pick_all, drift_x, ring_b, dampers_b, g0, h1, g2, late,
        in_sem, small_sem, xss, xrs, yss, yrs, css, crs, s_sem, r_sem, known,
    ) = refs[14:]
    gx = lax.axis_index("gx")
    gy = lax.axis_index("gy")
    f32, bf16 = jnp.float32, jnp.bfloat16

    def gx_peer(k):
        return {"gx": lax.rem(gx + k, NGX)}

    def gy_peer(k):
        return {"gy": lax.rem(gy + k, NGY)}

    barrier = pltpu.get_barrier_semaphore()

    plane, ring = gx // RX, lax.rem(gx, RX)

    def z_peer(k):
        return {"gx": lax.rem(plane + k, NGX // RX) * RX + ring}

    def x_peer(k):
        return {"gx": plane * RX + lax.rem(ring + k, RX)}

    nz = NGX // RX
    near = [gx_peer(1), gx_peer(NGX - 1)]
    near += [z_peer(k) for k in (1, nz - 1, 2, nz - 2)]
    near += [x_peer(k) for k in range(1, RX)]
    near += [gy_peer(k) for k in range(1, NGY)]
    ring_peers = [x_peer(k) for k in range(1, RX)]
    for peer in near:
        pl.semaphore_signal(barrier, 1, device_id=peer)

    def tell(i, peers):
        for peer in peers:
            pl.semaphore_signal(known.at[i], 1, device_id=peer)

    cv = pltpu.make_async_copy(vel_h, f0.at[0:3, 1 : 1 + CX, Y0 : Y0 + CY, :], in_sem.at[0])
    cp = pltpu.make_async_copy(pre_h, f0.at[3, 1 : 1 + CX, Y0 : Y0 + CY, :], in_sem.at[1])
    cn = pltpu.make_async_copy(vis_h, vis, in_sem.at[2])
    cv.start()
    cp.start()
    cn.start()
    small = [
        pltpu.make_async_copy(src, dst, small_sem.at[i])
        for i, (src, dst) in enumerate(
            zip(
                small_h,
                (wind, area, cell_s, cell_v, panels, shapes_t, nodes_t,
                 dnode, dvisc, dhyst, freq, ratio, modal, dstate),
            )
        )
    ]
    for c in small:
        c.start()
    cv.wait()
    cp.wait()

    y_order = (1, 0, 2, 3)

    def pack_x(f, p, comps):
        for k in comps:
            xs[p, 0, k] = f[k, CX, Y0 : Y0 + CY, :].astype(bf16)
            xs[p, 1, k] = f[k, 1, Y0 : Y0 + CY, :].astype(bf16)

    def pack_y(f, p, slots):
        for q in slots:
            k = y_order[q]
            for x in range(CX):
                ys[p, 0, q, x : x + 1, :] = f[k, x + 1, Y0 + CY - 1 : Y0 + CY, :]
                ys[p, 1, q, x : x + 1, :] = f[k, x + 1, Y0 : Y0 + 1, :]

    def x_copy(p, part, d, lo, hi):
        i = 2 * part + d
        return pltpu.make_async_remote_copy(
            xs.at[p, d, lo:hi], xr.at[p, d, lo:hi], xss.at[p, i], xrs.at[p, i],
            device_id=gx_peer(1 if d == 0 else NGX - 1),
        )

    def y_copy(p, part, d, lo, hi):
        i = 2 * part + d
        return pltpu.make_async_remote_copy(
            ys.at[p, d, lo:hi], yr.at[p, d, lo:hi], yss.at[p, i], yrs.at[p, i],
            device_id=gy_peer(1 if d == 0 else NGY - 1),
        )

    def unpack_x(f, p, comps):
        for k in comps:
            f[k, 0, Y0 : Y0 + CY, :] = jnp.where(gx == 0, 0.0, xr[p, 0, k].astype(f32))
            f[k, CX + 1, Y0 : Y0 + CY, :] = jnp.where(gx == NGX - 1, 0.0, xr[p, 1, k].astype(f32))

    def unpack_y(f, p, slots):
        for q in slots:
            k = y_order[q]
            for x in range(CX):
                f[k, x + 1, Y0 - 1 : Y0, :] = jnp.where(gy == 0, 0.0, yr[p, 0, q, x : x + 1, :])
                f[k, x + 1, Y0 + CY : Y0 + CY + 1, :] = jnp.where(
                    gy == NGY - 1, 0.0, yr[p, 1, q, x : x + 1, :]
                )

    lane8 = lax.broadcasted_iota(jnp.int32, (8, NZ), 1)

    def above(v):
        return jnp.where(lane8 == NZ - 1, 0.0, pltpu.roll(v, NZ - 1, 1))

    def below(v):
        return jnp.where(lane8 == 0, 0.0, pltpu.roll(v, 1, 1))

    small[0].wait()
    w_row = jnp.broadcast_to((-0.5 * time_step) * wind[...], (8, NZ))
    half = 0.5 * time_step

    x8 = lax.broadcasted_iota(jnp.int32, (CX, NZ), 0)

    def next_x(v):
        return jnp.where(x8 == CX - 1, 0.0, pltpu.roll(v, CX - 1, 0))

    def last_x(v):
        return jnp.where(x8 == 0, 0.0, pltpu.roll(v, 1, 0))

    def outer_x(d):
        x, inner, sign = (CX, CX - 1, 1.0) if d == 0 else (1, 2, -1.0)
        zero = jnp.zeros((1, NZ), f32)
        f0[0, x, Y0 - 1 : Y0, :] = zero
        f0[0, x, Y0 + CY : Y0 + CY + 1, :] = zero
        for t in range(YT):
            rows = pl.ds(Y0 + 8 * t, 8)
            own = slice(8 * t, 8 * t + 8)
            c, i, p = f0[0, x, rows, :], f0[0, inner, rows, :], f0[3, inner, rows, :]
            r, l = f0[0, x, pl.ds(Y0 + 8 * t + 1, 8), :], f0[0, x, pl.ds(Y0 + 8 * t - 1, 8), :]
            lap = (i + (r + l)) + ((above(c) + below(c)) - 6.0 * c)
            nu = time_step * vis[x - 1, own, :]
            tile = c + (nu * lap + sign * (half * p - w_row * i))
            yield own, tile, vis[x - 1, own, :]

    def pack_outer_x():
        for d in range(2):
            for own, tile, nu in outer_x(d):
                xs[0, d, 4, own, :] = tile.astype(bf16)
                xs[0, d, 5, own, :] = nu.astype(bf16)

    def pack_outer_y():
        for d in range(2):
            y, inner, sign = (Y0 + CY - 1, Y0 + CY - 2, 1.0) if d == 0 else (Y0, Y0 + 1, -1.0)
            for x in range(CX):
                yi[d, 0, x : x + 1, :] = f0[1, x + 1, inner : inner + 1, :]
                yi[d, 1, x : x + 1, :] = f0[3, x + 1, inner : inner + 1, :]
                ys[0, d, 5, x : x + 1, :] = vis[x, y - Y0 : y - Y0 + 1, :]
            c, nu = ys[0, d, 0], time_step * ys[0, d, 5]
            a, b = next_x(c), last_x(c)
            lap = (yi[d, 0] + (a + b)) + ((above(c) + below(c)) - 6.0 * c)
            ys[0, d, 4] = c + (w_row * (a - b) + nu * lap + (sign * half) * yi[d, 1])

    pack_y(f0, 0, range(4))
    cn.wait()
    pack_outer_y()
    pack_x(f0, 0, range(4))
    pack_outer_x()
    pl.semaphore_wait(barrier, len(near))
    tell(0, [z_peer(2), z_peer(nz - 2)] + ring_peers)
    hx1 = [x_copy(0, 0, d, 0, 6) for d in range(2)]
    hy1 = [y_copy(0, 0, d, 0, 6) for d in range(2)]
    for c in hy1 + hx1:
        c.start()

    for c in small[1:]:
        c.wait()
    dn = dnode[...].astype(f32)
    dn2 = twice(dn)
    node_no = lax.broadcasted_iota(jnp.int32, (nodes_t.shape[1], 2 * DB), 0).astype(f32)

    def pick(row):
        return jnp.where(node_no == row + 1.0, 1.0, jnp.where(node_no == row, -1.0, 0.0)).astype(bf16)

    drift = jnp.dot(nodes_t[...], pick(dn2), preferred_element_type=f32)
    q0 = column_of(modal[0:1, :], MB)
    v0 = column_of(modal[1:2, :], MB)
    first_half = lax.broadcasted_iota(jnp.int32, (MB, 2 * DB), 1) < DB
    odd = lax.rem(gy, 2)
    own_half = (lax.broadcasted_iota(jnp.int32, (1, 2 * DB), 1) // DB) == odd

    def placed_half(row):
        return jnp.where(own_half, twice(row), 0.0)

    dampers_b[gy, 0:1, :] = placed_half(dvisc[...])
    dampers_b[gy, 1:2, :] = placed_half(dhyst[...])
    dampers_b[gy, 2:3, :] = placed_half(dn)
    ring_b[ring, 0:1, :] = jnp.sum(
        drift * jnp.where(first_half, q0, v0), axis=0, keepdims=True
    )
    ring_b[ring, 1:2, :] = row_of(q0, MB * ring)
    ring_b[ring, 2:3, :] = row_of(v0, MB * ring)
    ring_b[ring, 3:4, :] = row_of(column_of(freq[...], MB), MB * ring)
    ring_b[ring, 4:5, :] = row_of(column_of(ratio[...], MB), MB * ring)

    def spread(buf, me, peers, sem_no):
        for peer in peers:
            pltpu.make_async_remote_copy(
                buf.at[me], buf.at[me], s_sem.at[sem_no], r_sem.at[sem_no], device_id=peer
            ).start()
        most = buf.at[pl.ds(0, len(peers))]
        return pltpu.make_async_remote_copy(
            most, most, s_sem.at[sem_no], r_sem.at[sem_no], device_id=peers[0]
        )

    def far_first(n):
        return sorted(range(n), key=lambda k: -min(k, n - k))

    z_peers = [z_peer(k) for k in far_first(nz)[:-1]]
    gy_peers = [gy_peer(k) for k in far_first(NGY)[:-1]]
    x_peers = [x_peer(k) for k in far_first(RX)[:-1]]

    ring_stage = spread(ring_b, ring, x_peers, 0)
    damper_stage = spread(dampers_b, gy, gy_peers, 1)

    parity = lax.rem(gx, 2)
    own_ids = column_of(panels[pl.ds(gx // 2, 1), :], SL, SL * parity)
    panel_no = lax.broadcasted_iota(jnp.int32, (SL, area.shape[1]), 1)
    own_area = jnp.sum(jnp.where(panel_no == own_ids, area[...], 0.0), axis=1, keepdims=True)
    own_z = column_of(cell_v[...], SL) & (NZ - 1)
    z_mask = (lax.broadcasted_iota(jnp.int32, (SL, NZ), 1) == own_z)

    def velocity_tile(f, x, t):
        rows = pl.ds(Y0 + 8 * t, 8)
        rows_m = pl.ds(Y0 + 8 * t - 1, 8)
        rows_p = pl.ds(Y0 + 8 * t + 1, 8)
        nu = time_step * vis[x - 1, 8 * t : 8 * t + 8, :]
        pc = f[3, x, rows, :]
        slope = (
            f[3, x + 1, rows, :] - f[3, x - 1, rows, :],
            f[3, x, rows_p, :] - f[3, x, rows_m, :],
            above(pc) - below(pc),
        )
        out = []
        for k in range(3):
            c = f[k, x, rows, :]
            a, b = f[k, x + 1, rows, :], f[k, x - 1, rows, :]
            r, l = f[k, x, rows_p, :], f[k, x, rows_m, :]
            u, d = above(c), below(c)
            lap = ((a + b) + (r + l)) + ((u + d) - 6.0 * c)
            out.append(c + (w_row * (a - b) + nu * lap - half * slope[k]))
        return out

    def pressure_tile(f, x, t):
        rows = pl.ds(Y0 + 8 * t, 8)
        rows_m = pl.ds(Y0 + 8 * t - 1, 8)
        rows_p = pl.ds(Y0 + 8 * t + 1, 8)
        w = f[2, x, rows, :]
        div = (f[0, x + 1, rows, :] - f[0, x - 1, rows, :]) + (
            (f[1, x, rows_p, :] - f[1, x, rows_m, :]) + (above(w) - below(w))
        )
        return f[3, x, rows, :] - (half * sound_squared) * div

    def first_layer(x, carry):
        for t in range(YT):
            rows = slice(Y0 + 8 * t, Y0 + 8 * t + 8)
            new = velocity_tile(f0, x, t)
            for k in range(3):
                f1[k, x, rows, :] = new[k]
            f1[3, x, rows, :] = pressure_tile(f0, x, t)
        return carry

    shapes_x[ring] = shapes_t[...]
    nodes_x[ring] = nodes_t[...]
    for c in hy1:
        c.wait_recv()
    corners = []
    for d in range(2):
        x = CX - 1 if d == 0 else 0
        for side in range(2):
            for q in range(2):
                i = 2 * side + q
                cs[d, i : i + 1, :] = yr[0, side, q, x : x + 1, :]
        corners.append(
            pltpu.make_async_remote_copy(
                cs.at[d], cr.at[d], css.at[d], crs.at[d],
                device_id=gx_peer(1 if d == 0 else NGX - 1),
            )
        )
        corners[d].start()
    unpack_y(f0, 0, range(4))
    pl.semaphore_wait(known.at[0], 2 + len(ring_peers))
    tell(1, [z_peer(4), z_peer(nz - 4)])
    lax.fori_loop(2, CX, first_layer, 0)
    for c in hx1:
        c.wait_recv()
    shapes_stage = spread(shapes_x, ring, x_peers, 2)
    unpack_x(f0, 0, range(4))
    first_layer(1, 0)
    first_layer(CX, 0)


    for c in corners:
        c.wait_recv()
    for d in range(2):
        x, far, sign = (1, 0, 1.0) if d == 0 else (CX, CX + 1, -1.0)
        edge = gx == (0 if d == 0 else NGX - 1)
        for t in range(YT):
            rows, own = slice(Y0 + 8 * t, Y0 + 8 * t + 8), slice(8 * t, 8 * t + 8)
            u, p = f0[0, x, rows, :], f0[3, x, rows, :]
            nu = time_step * xr[0, d, 5, own, :].astype(f32)
            tile = xr[0, d, 4, own, :].astype(f32) + (nu * u + sign * (w_row * u - half * p))
            if t == 0:
                corner = jnp.where(gy == 0, 0.0, cr[d, 1:2, :])
                tile = tile + jnp.where(x8 == 0, nu * corner, 0.0)
            if t == YT - 1:
                corner = jnp.where(gy == NGY - 1, 0.0, cr[d, 3:4, :])
                tile = tile + jnp.where(x8 == 7, nu * corner, 0.0)
            f1[0, far, rows, :] = jnp.where(edge, 0.0, tile)
    for d in range(2):
        sign = 1.0 if d == 0 else -1.0
        edge = gy == (0 if d == 0 else NGY - 1)
        u, p = ys[0, 1 - d, 0], ys[0, 1 - d, 3]
        nu = time_step * yr[0, d, 5]
        low = jnp.where(gx == 0, 0.0, cr[0, 2 * d : 2 * d + 1, :])
        high = jnp.where(gx == NGX - 1, 0.0, cr[1, 2 * d : 2 * d + 1, :])
        tile = yr[0, d, 4] + (nu * u - (sign * half) * p)
        tile = tile + jnp.where(x8 == 0, (nu - w_row) * low, 0.0)
        tile = tile + jnp.where(x8 == CX - 1, (nu + w_row) * high, 0.0)
        yi[d, 0] = jnp.where(edge, 0.0, tile)
        y = Y0 - 1 if d == 0 else Y0 + CY
        for x in range(CX):
            f1[1, x + 1, y : y + 1, :] = yi[d, 0, x : x + 1, :]

    def second_pressure(x, carry):
        for t in range(YT):
            pre_o[x - 1, 8 * t : 8 * t + 8, :] = pressure_tile(f1, x, t)
        return carry

    lax.fori_loop(1, CX + 1, second_pressure, 0)

    for s in range(SL):
        line = cell_s[0, s] >> 8
        layer = line // CY
        samp[s : s + 1, :] = pre_o[layer, pl.ds(line - layer * CY, 1), :]
    sampled = jnp.sum(jnp.where(z_mask, samp[...], 0.0), axis=1, keepdims=True)
    load = (own_area * sampled).astype(bf16).astype(f32)
    g0[plane, 0:1, :] = row_of(load, SL * parity)
    ring_stage.wait_recv()
    g0[plane, 1:2, :] = jnp.sum(ring_b[:, 0:1, :], axis=0)
    pl.semaphore_wait(known.at[1], 2)
    stage0 = spread(g0, plane, z_peers, 3)
    for c in hx1 + hy1 + corners + [ring_stage, damper_stage]:
        c.wait_send()
    damper_stage.wait_recv()

    def table(i, carry):
        low = panels[pl.ds(2 * i + ring // 2, 1), :] & 127
        sub = lax.broadcasted_iota(jnp.int32, (128, 128), 0)
        onehot[:, pl.ds(pl.multiple_of(i * 128, 128), 128)] = (sub == low).astype(f32).astype(bf16)
        return carry

    lax.fori_loop(0, nz, table, 0)

    def paired(buf, row):
        return jnp.concatenate(
            [buf[2 * j, row : row + 1, :] + buf[2 * j + 1, row : row + 1, :] for j in range(NGY // 2)],
            axis=0,
        )

    visc_all, hyst_all, node_all = (paired(dampers_b, r) for r in range(3))
    for j in range(NGY // 2):
        pick_all[:, j * 128 : (j + 1) * 128] = pick(node_all[j : j + 1, :])
    q0_row, v0_row, omega, zeta = (jnp.sum(ring_b[:, r : r + 1, :], axis=0) for r in range(1, 5))

    shapes_stage.wait_recv()
    nodes_stage = spread(nodes_x, ring, x_peers, 4)
    stage0.wait_recv()
    sub16 = lax.broadcasted_iota(jnp.int32, (16, 128), 0)
    for i in range(nz):
        high = panels[pl.ds(2 * i + ring // 2, 1), :] >> 7
        lhs[:, i * 128 : (i + 1) * 128] = jnp.where(sub16 == high, g0[i, 0:1, :], 0.0).astype(bf16)
    placed = lax.dot_general(
        lhs[...], onehot[...], (((1,), (1,)), ((), ())), preferred_element_type=f32
    )
    parts = []
    for r in range(RX):
        part = jnp.zeros((MB, 128), f32)
        for a in range(16):
            part = part + shapes_x[r, :, a * 128 : (a + 1) * 128].astype(f32) * placed[a : a + 1, :]
        parts.append(row_of(jnp.sum(part, axis=1, keepdims=True), MB * r))

    def response(stretch, rate, viscous, hysteretic, hysteresis):
        hysteresis = hysteresis + modal_step * (
            hysteresis_gain * rate
            - shape_beta * jnp.abs(rate) * hysteresis
            - shape_gamma * rate * jnp.abs(hysteresis)
        )
        return hysteresis, -(viscous * rate + spring_rate * stretch + hysteretic * hysteresis)

    first = jnp.sum(g0[:, 1:2, :], axis=0)
    stretch0 = first[:, 0:DB]
    hysteresis, force = response(stretch0, first[:, DB : 2 * DB], dvisc[...], dhyst[...], dstate[...])
    damper_part = jnp.sum(drift[:, 0:DB] * force, axis=1, keepdims=True)
    spot = ring * NGY + gy
    h1[spot, 0:1, :] = (parts[0] + parts[1]) + (parts[2] + parts[3])
    h1[spot, 1:2, :] = row_of(damper_part, MB * ring)
    h1[spot, 2:3, :] = placed_half(stretch0)
    h1[spot, 3:4, :] = placed_half(hysteresis)

    plane_peers = []
    steps = [(a, b, c) for a in range(RX) for b in range(NGY // 2) for c in range(2)]
    for a, b, c in sorted(steps, key=lambda k: -min(k[0], RX - k[0]) - min(k[1], NGY // 2 - k[1])):
        if a or b or c:
            there = 2 * lax.rem(gy // 2 + b, NGY // 2) + lax.rem(odd + c, 2)
            plane_peers.append({"gx": plane * RX + lax.rem(ring + a, RX), "gy": there})
    stage1 = spread(h1, spot, plane_peers, 5)
    stage0.wait_send()
    shapes_stage.wait_send()
    nodes_stage.wait_recv()
    drift_x[...] = jnp.dot(
        nodes_x[...].reshape(RX * MB, -1), pick_all[...], preferred_element_type=f32
    )
    pack_x(f1, 1, (1, 2, 3))
    pack_y(f1, 1, (1, 2, 3))
    hx3 = [x_copy(1, 1, d, 1, 4) for d in range(2)]
    hy3 = [y_copy(1, 1, d, 1, 4) for d in range(2)]
    for c in hx3 + hy3:
        c.start()
    nodes_stage.wait_send()
    stage1.wait_recv()
    panel_modal = jnp.sum(h1[:, 0:1, :], axis=0)
    damper_modal = jnp.sum(h1[:, 1:2, :], axis=0)
    stretch_all, hysteresis_all = paired(h1, 2), paired(h1, 3)

    def advance_modes(q, v, damper_load):
        acceleration = (
            panel_modal + damper_load - 2.0 * zeta * omega * v - omega * omega * q
        )
        v = v + modal_step * acceleration
        return q + modal_step * v, v

    q1, v1 = advance_modes(q0_row, v0_row, damper_modal)
    v1_column = column_of(v1, RX * MB)
    for j in range(NGY // 2):
        g2[plane, j : j + 1, :] = jnp.sum(
            drift_x[:, j * 128 : (j + 1) * 128] * v1_column, axis=0, keepdims=True
        )
    stage2 = spread(g2, plane, z_peers, 6)
    stage1.wait_send()
    for c in hx3 + hy3:
        c.wait_recv()
    unpack_x(f1, 1, (1, 2, 3))
    unpack_y(f1, 1, (1, 2, 3))

    def second_velocity(x, carry):
        for t in range(YT):
            new = velocity_tile(f1, x, t)
            for k in range(3):
                vel_o[k, x - 1, 8 * t : 8 * t + 8, :] = new[k]
        return carry

    lax.fori_loop(1, CX + 1, second_velocity, 0)
    for c in hx3 + hy3:
        c.wait_send()
    stage2.wait_recv()
    rate_all = jnp.sum(g2[...], axis=0)
    stretch_all = stretch_all + modal_step * rate_all
    hysteresis_all, force = response(stretch_all, rate_all, visc_all, hyst_all, hysteresis_all)
    late[...] = hysteresis_all
    own = late[pl.ds(gy // 2, 1), :]
    damp_o[...] = jnp.where(odd == 1, own[:, DB : 2 * DB], own[:, 0:DB])
    part = jnp.zeros((MB, 128), f32)
    for j in range(NGY // 2):
        rows = pl.ds(pl.multiple_of(ring * MB, MB), MB)
        part = part + drift_x[rows, j * 128 : (j + 1) * 128] * force[j : j + 1, :]
    damper_modal = row_of(jnp.sum(part, axis=1, keepdims=True), MB * ring)
    q2, v2 = advance_modes(q1, v1, damper_modal)
    modal_o[0:1, :] = row_of(column_of(q2, MB, MB * ring), 0, MB)
    modal_o[1:2, :] = row_of(column_of(v2, MB, MB * ring), 0, MB)
    stage2.wait_send()


def write_out(*refs):
    n = len(refs) // 2
    sem = refs[-1]
    copies = [pltpu.make_async_copy(refs[i], refs[n + i], sem.at[i]) for i in range(n)]
    for c in copies:
        c.start()
    for c in copies:
        c.wait()


def body(
    velocity, pressure, viscosity, wind_profile, panel_area, slot_cell, slot_panel, panel_shapes,
    node_shapes, damper_node, damper_viscous, damper_hysteretic, frequency, damping_ratio,
    modal_state, damper_state,
):
    hbm = pl.BlockSpec(memory_space=pltpu.MemorySpace.HBM)
    vmem = pl.BlockSpec(memory_space=pltpu.VMEM)
    f32, bf16 = jnp.float32, jnp.bfloat16
    slots = slot_panel.shape[1]
    small = (
        wind_profile.reshape(1, -1), panel_area.reshape(1, -1),
        slot_cell, slot_cell, slot_panel.reshape(slots // 128, 128), panel_shapes.T, node_shapes.T,
        damper_node.reshape(1, -1), damper_viscous.reshape(1, -1), damper_hysteretic.reshape(1, -1),
        frequency.reshape(1, -1), damping_ratio.reshape(1, -1), modal_state,
        damper_state.reshape(1, -1),
    )
    outs = (
        jax.ShapeDtypeStruct(velocity.shape, f32),
        jax.ShapeDtypeStruct(pressure.shape, f32),
        jax.ShapeDtypeStruct(modal_state.shape, f32),
        jax.ShapeDtypeStruct((1, DB), f32),
    )
    held = [
        (pltpu.SMEM if i == 2 else pltpu.VMEM)(a.shape, a.dtype) for i, a in enumerate(small)
    ]
    results = pl.pallas_call(
        kernel,
        out_shape=outs,
        in_specs=[hbm] * (3 + len(small)),
        out_specs=(vmem,) * 4,
        scratch_shapes=held + [
            pltpu.VMEM((4, CX + 2, CY + 16, NZ), f32),
            pltpu.VMEM((4, CX + 2, CY + 16, NZ), f32),
            pltpu.VMEM((CX, CY, NZ), f32),
            pltpu.VMEM((2, 2, 6, CY, NZ), bf16),
            pltpu.VMEM((2, 2, 6, CY, NZ), bf16),
            pltpu.VMEM((2, 2, 6, CX, NZ), f32),
            pltpu.VMEM((2, 2, 6, CX, NZ), f32),
            pltpu.VMEM((2, 2, CX, NZ), f32),
            pltpu.VMEM((2, 4, NZ), f32),
            pltpu.VMEM((2, 4, NZ), f32),
            pltpu.VMEM((SL, NZ), f32),
            pltpu.VMEM((128, NGX // RX * 128), bf16),
            pltpu.VMEM((16, NGX // RX * 128), bf16),
            pltpu.VMEM((RX,) + panel_shapes.shape[::-1], bf16),
            pltpu.VMEM((RX,) + node_shapes.shape[::-1], bf16),
            pltpu.VMEM((node_shapes.shape[0], DB * NGY), bf16),
            pltpu.VMEM((RX * MB, DB * NGY), f32),
            pltpu.VMEM((RX, 8, 128), f32),
            pltpu.VMEM((NGY, 4, 128), f32),
            pltpu.VMEM((NGX // RX, 2, 128), f32),
            pltpu.VMEM((RX * NGY, 4, 128), f32),
            pltpu.VMEM((NGX // RX, NGY // 2, 128), f32),
            pltpu.VMEM((NGY // 2, 128), f32),
            pltpu.SemaphoreType.DMA((3,)),
            pltpu.SemaphoreType.DMA((len(small),)),
            pltpu.SemaphoreType.DMA((2, 4)),
            pltpu.SemaphoreType.DMA((2, 4)),
            pltpu.SemaphoreType.DMA((2, 4)),
            pltpu.SemaphoreType.DMA((2, 4)),
            pltpu.SemaphoreType.DMA((2,)),
            pltpu.SemaphoreType.DMA((2,)),
            pltpu.SemaphoreType.DMA((7,)),
            pltpu.SemaphoreType.DMA((7,)),
            pltpu.SemaphoreType.REGULAR((2,)),
        ],
        compiler_params=pltpu.CompilerParams(
            collective_id=0, has_side_effects=True, vmem_limit_bytes=40 << 20
        ),
    )(*[pltpu.with_memory_space_constraint(a, pltpu.MemorySpace.HBM) for a in (velocity, pressure, viscosity, *small)])
    vel, pre, modal, damp = pl.pallas_call(
        write_out,
        out_shape=outs,
        in_specs=[vmem] * 4,
        out_specs=(hbm,) * 4,
        scratch_shapes=[pltpu.SemaphoreType.DMA((4,))], compiler_params=pltpu.CompilerParams(vmem_limit_bytes=1 << 20),
    )(*results)
    return vel, pre, modal, damp.reshape(-1)


def solution(mesh):
    placed = (
        P(None, "gx", "gy", None),
        P("gx", "gy", None),
        P("gx", "gy", None),
        P(),
        P("gy"),
        P("gy", "gx"),
        P("gy", None),
        P("gy", "gx"),
        P(None, "gx"),
        P("gy"),
        P("gy"),
        P("gy"),
        P("gx"),
        P("gx"),
        P(None, "gx"),
        P("gy"),
    )
    return jax.shard_map(
        body,
        mesh=mesh,
        in_specs=placed,
        out_specs=(P(None, "gx", "gy", None), P("gx", "gy", None), P(None, "gx"), P("gy")),
        check_vma=False,
    )
```

```python
import jax
import jax.numpy as jnp
from jax import lax
from jax.experimental import pallas as pl
from jax.experimental.pallas import tpu as pltpu
from jax.sharding import PartitionSpec as P

time_step = 0.1
sound_squared = 1.0
modal_step = 0.5
hysteresis_gain = 1.0
shape_beta = 0.5
shape_gamma = 0.5
spring_rate = 0.5

CX, CY, NZ = 8, 48, 256
NGX, NGY = 64, 8
RX = 4
MB = 32
DB = 64
SL = 64
Y0 = 8
YT = CY // 8


def row_of(column, lane_shift=0, lanes=128):
    n = column.shape[0]
    sub = lax.broadcasted_iota(jnp.int32, (n, lanes), 0)
    lane = lax.broadcasted_iota(jnp.int32, (n, lanes), 1)
    return jnp.sum(jnp.where(lane == sub + lane_shift, column, 0.0), axis=0, keepdims=True)


def column_of(row, n, lane_shift=0):
    lanes = row.shape[1]
    sub = lax.broadcasted_iota(jnp.int32, (n, lanes), 0)
    lane = lax.broadcasted_iota(jnp.int32, (n, lanes), 1)
    zero = jnp.zeros((), row.dtype)
    return jnp.sum(jnp.where(lane == sub + lane_shift, row, zero), axis=1, keepdims=True)


def twice(row):
    return jnp.concatenate([row, row], axis=1)


def kernel(
    vel_h, pre_h, vis_h, *refs,
):
    small_h = refs[:14]
    (
        vel_o, pre_o, modal_o, damp_o,
        wind, area, cell_s, cell_v, panels, shapes_t, nodes_t,
        dnode, dvisc, dhyst, freq, ratio, modal, dstate,
        f0, f1, vis, xs, xr, ys, yr, yi, cs, cr, samp, onehot, lhs,
        shapes_x, nodes_x, pick_all, drift_x, ring_b, dampers_b, g0, h1, g2, late,
        in_sem, small_sem, xss, xrs, yss, yrs, css, crs, s_sem, r_sem, known,
    ) = refs[14:]
    gx = lax.axis_index("gx")
    gy = lax.axis_index("gy")
    f32, bf16 = jnp.float32, jnp.bfloat16

    def gx_peer(k):
        return {"gx": lax.rem(gx + k, NGX)}

    def gy_peer(k):
        return {"gy": lax.rem(gy + k, NGY)}

    barrier = pltpu.get_barrier_semaphore()

    plane, ring = gx // RX, lax.rem(gx, RX)

    def z_peer(k):
        return {"gx": lax.rem(plane + k, NGX // RX) * RX + ring}

    def x_peer(k):
        return {"gx": plane * RX + lax.rem(ring + k, RX)}

    nz = NGX // RX
    near = [gx_peer(1), gx_peer(NGX - 1)]
    near += [z_peer(k) for k in (1, nz - 1, 2, nz - 2)]
    near += [x_peer(k) for k in range(1, RX)]
    near += [gy_peer(k) for k in range(1, NGY)]
    ring_peers = [x_peer(k) for k in range(1, RX)]
    for peer in near:
        pl.semaphore_signal(barrier, 1, device_id=peer)

    def tell(i, peers):
        for peer in peers:
            pl.semaphore_signal(known.at[i], 1, device_id=peer)

    cv = pltpu.make_async_copy(vel_h, f0.at[0:3, 1 : 1 + CX, Y0 : Y0 + CY, :], in_sem.at[0])
    cp = pltpu.make_async_copy(pre_h, f0.at[3, 1 : 1 + CX, Y0 : Y0 + CY, :], in_sem.at[1])
    cn = pltpu.make_async_copy(vis_h, vis, in_sem.at[2])
    cv.start()
    cp.start()
    cn.start()
    small = [
        pltpu.make_async_copy(src, dst, small_sem.at[i])
        for i, (src, dst) in enumerate(
            zip(
                small_h,
                (wind, area, cell_s, cell_v, panels, shapes_t, nodes_t,
                 dnode, dvisc, dhyst, freq, ratio, modal, dstate),
            )
        )
    ]
    for c in small:
        c.start()
    cv.wait()
    cp.wait()

    y_order = (1, 0, 2, 3)

    def pack_x(f, p, comps):
        for k in comps:
            xs[p, 0, k] = f[k, CX, Y0 : Y0 + CY, :].astype(bf16)
            xs[p, 1, k] = f[k, 1, Y0 : Y0 + CY, :].astype(bf16)

    def pack_y(f, p, slots):
        for q in slots:
            k = y_order[q]
            for x in range(CX):
                ys[p, 0, q, x : x + 1, :] = f[k, x + 1, Y0 + CY - 1 : Y0 + CY, :]
                ys[p, 1, q, x : x + 1, :] = f[k, x + 1, Y0 : Y0 + 1, :]

    def x_copy(p, part, d, lo, hi):
        i = 2 * part + d
        return pltpu.make_async_remote_copy(
            xs.at[p, d, lo:hi], xr.at[p, d, lo:hi], xss.at[p, i], xrs.at[p, i],
            device_id=gx_peer(1 if d == 0 else NGX - 1),
        )

    def y_copy(p, part, d, lo, hi):
        i = 2 * part + d
        return pltpu.make_async_remote_copy(
            ys.at[p, d, lo:hi], yr.at[p, d, lo:hi], yss.at[p, i], yrs.at[p, i],
            device_id=gy_peer(1 if d == 0 else NGY - 1),
        )

    def unpack_x(f, p, comps):
        for k in comps:
            f[k, 0, Y0 : Y0 + CY, :] = jnp.where(gx == 0, 0.0, xr[p, 0, k].astype(f32))
            f[k, CX + 1, Y0 : Y0 + CY, :] = jnp.where(gx == NGX - 1, 0.0, xr[p, 1, k].astype(f32))

    def unpack_y(f, p, slots):
        for q in slots:
            k = y_order[q]
            for x in range(CX):
                f[k, x + 1, Y0 - 1 : Y0, :] = jnp.where(gy == 0, 0.0, yr[p, 0, q, x : x + 1, :])
                f[k, x + 1, Y0 + CY : Y0 + CY + 1, :] = jnp.where(
                    gy == NGY - 1, 0.0, yr[p, 1, q, x : x + 1, :]
                )

    lane8 = lax.broadcasted_iota(jnp.int32, (8, NZ), 1)

    def above(v):
        return jnp.where(lane8 == NZ - 1, 0.0, pltpu.roll(v, NZ - 1, 1))

    def below(v):
        return jnp.where(lane8 == 0, 0.0, pltpu.roll(v, 1, 1))

    small[0].wait()
    w_row = jnp.broadcast_to((-0.5 * time_step) * wind[...], (8, NZ))
    half = 0.5 * time_step

    x8 = lax.broadcasted_iota(jnp.int32, (CX, NZ), 0)

    def next_x(v):
        return jnp.where(x8 == CX - 1, 0.0, pltpu.roll(v, CX - 1, 0))

    def last_x(v):
        return jnp.where(x8 == 0, 0.0, pltpu.roll(v, 1, 0))

    def outer_x(d):
        x, inner, sign = (CX, CX - 1, 1.0) if d == 0 else (1, 2, -1.0)
        zero = jnp.zeros((1, NZ), f32)
        f0[0, x, Y0 - 1 : Y0, :] = zero
        f0[0, x, Y0 + CY : Y0 + CY + 1, :] = zero
        for t in range(YT):
            rows = pl.ds(Y0 + 8 * t, 8)
            own = slice(8 * t, 8 * t + 8)
            c, i, p = f0[0, x, rows, :], f0[0, inner, rows, :], f0[3, inner, rows, :]
            r, l = f0[0, x, pl.ds(Y0 + 8 * t + 1, 8), :], f0[0, x, pl.ds(Y0 + 8 * t - 1, 8), :]
            lap = (i + (r + l)) + ((above(c) + below(c)) - 6.0 * c)
            nu = time_step * vis[x - 1, own, :]
            tile = c + (nu * lap + sign * (half * p - w_row * i))
            yield own, tile, vis[x - 1, own, :]

    def pack_outer_x():
        for d in range(2):
            for own, tile, nu in outer_x(d):
                xs[0, d, 4, own, :] = tile.astype(bf16)
                xs[0, d, 5, own, :] = nu.astype(bf16)

    def pack_outer_y():
        for d in range(2):
            y, inner, sign = (Y0 + CY - 1, Y0 + CY - 2, 1.0) if d == 0 else (Y0, Y0 + 1, -1.0)
            for x in range(CX):
                yi[d, 0, x : x + 1, :] = f0[1, x + 1, inner : inner + 1, :]
                yi[d, 1, x : x + 1, :] = f0[3, x + 1, inner : inner + 1, :]
                ys[0, d, 5, x : x + 1, :] = vis[x, y - Y0 : y - Y0 + 1, :]
            c, nu = ys[0, d, 0], time_step * ys[0, d, 5]
            a, b = next_x(c), last_x(c)
            lap = (yi[d, 0] + (a + b)) + ((above(c) + below(c)) - 6.0 * c)
            ys[0, d, 4] = c + (w_row * (a - b) + nu * lap + (sign * half) * yi[d, 1])

    pack_y(f0, 0, range(4))
    cn.wait()
    pack_outer_y()
    pack_x(f0, 0, range(4))
    pack_outer_x()
    pl.semaphore_wait(barrier, len(near))
    tell(0, [z_peer(2), z_peer(nz - 2)] + ring_peers)
    hx1 = [x_copy(0, 0, d, 0, 6) for d in range(2)]
    hy1 = [y_copy(0, 0, d, 0, 6) for d in range(2)]
    for c in hy1 + hx1:
        c.start()

    for c in small[1:]:
        c.wait()
    dn = dnode[...].astype(f32)
    dn2 = twice(dn)
    node_no = lax.broadcasted_iota(jnp.int32, (nodes_t.shape[1], 2 * DB), 0).astype(f32)

    def pick(row):
        return jnp.where(node_no == row + 1.0, 1.0, jnp.where(node_no == row, -1.0, 0.0)).astype(bf16)

    drift = jnp.dot(nodes_t[...], pick(dn2), preferred_element_type=f32)
    q0 = column_of(modal[0:1, :], MB)
    v0 = column_of(modal[1:2, :], MB)
    first_half = lax.broadcasted_iota(jnp.int32, (MB, 2 * DB), 1) < DB
    odd = lax.rem(gy, 2)
    own_half = (lax.broadcasted_iota(jnp.int32, (1, 2 * DB), 1) // DB) == odd

    def placed_half(row):
        return jnp.where(own_half, twice(row), 0.0)

    dampers_b[gy, 0:1, :] = placed_half(dvisc[...])
    dampers_b[gy, 1:2, :] = placed_half(dhyst[...])
    dampers_b[gy, 2:3, :] = placed_half(dn)
    ring_b[ring, 0:1, :] = jnp.sum(
        drift * jnp.where(first_half, q0, v0), axis=0, keepdims=True
    )
    ring_b[ring, 1:2, :] = row_of(q0, MB * ring)
    ring_b[ring, 2:3, :] = row_of(v0, MB * ring)
    ring_b[ring, 3:4, :] = row_of(column_of(freq[...], MB), MB * ring)
    ring_b[ring, 4:5, :] = row_of(column_of(ratio[...], MB), MB * ring)

    def spread(buf, me, peers, sem_no):
        for peer in peers:
            pltpu.make_async_remote_copy(
                buf.at[me], buf.at[me], s_sem.at[sem_no], r_sem.at[sem_no], device_id=peer
            ).start()
        most = buf.at[pl.ds(0, len(peers))]
        return pltpu.make_async_remote_copy(
            most, most, s_sem.at[sem_no], r_sem.at[sem_no], device_id=peers[0]
        )

    def far_first(n):
        return sorted(range(n), key=lambda k: -min(k, n - k))

    z_peers = [z_peer(k) for k in far_first(nz)[:-1]]
    gy_peers = [gy_peer(k) for k in far_first(NGY)[:-1]]
    x_peers = [x_peer(k) for k in far_first(RX)[:-1]]

    ring_stage = spread(ring_b, ring, x_peers, 0)
    damper_stage = spread(dampers_b, gy, gy_peers, 1)

    parity = lax.rem(gx, 2)
    own_ids = column_of(panels[pl.ds(gx // 2, 1), :], SL, SL * parity)
    panel_no = lax.broadcasted_iota(jnp.int32, (SL, area.shape[1]), 1)
    own_area = jnp.sum(jnp.where(panel_no == own_ids, area[...], 0.0), axis=1, keepdims=True)
    own_z = column_of(cell_v[...], SL) & (NZ - 1)
    z_mask = (lax.broadcasted_iota(jnp.int32, (SL, NZ), 1) == own_z)

    def velocity_tile(f, x, t):
        rows = pl.ds(Y0 + 8 * t, 8)
        rows_m = pl.ds(Y0 + 8 * t - 1, 8)
        rows_p = pl.ds(Y0 + 8 * t + 1, 8)
        nu = time_step * vis[x - 1, 8 * t : 8 * t + 8, :]
        pc = f[3, x, rows, :]
        slope = (
            f[3, x + 1, rows, :] - f[3, x - 1, rows, :],
            f[3, x, rows_p, :] - f[3, x, rows_m, :],
            above(pc) - below(pc),
        )
        out = []
        for k in range(3):
            c = f[k, x, rows, :]
            a, b = f[k, x + 1, rows, :], f[k, x - 1, rows, :]
            r, l = f[k, x, rows_p, :], f[k, x, rows_m, :]
            u, d = above(c), below(c)
            lap = ((a + b) + (r + l)) + ((u + d) - 6.0 * c)
            out.append(c + (w_row * (a - b) + nu * lap - half * slope[k]))
        return out

    def pressure_tile(f, x, t):
        rows = pl.ds(Y0 + 8 * t, 8)
        rows_m = pl.ds(Y0 + 8 * t - 1, 8)
        rows_p = pl.ds(Y0 + 8 * t + 1, 8)
        w = f[2, x, rows, :]
        div = (f[0, x + 1, rows, :] - f[0, x - 1, rows, :]) + (
            (f[1, x, rows_p, :] - f[1, x, rows_m, :]) + (above(w) - below(w))
        )
        return f[3, x, rows, :] - (half * sound_squared) * div

    def first_layer(x, carry):
        for t in range(YT):
            rows = slice(Y0 + 8 * t, Y0 + 8 * t + 8)
            new = velocity_tile(f0, x, t)
            for k in range(3):
                f1[k, x, rows, :] = new[k]
            f1[3, x, rows, :] = pressure_tile(f0, x, t)
        return carry

    shapes_x[ring] = shapes_t[...]
    nodes_x[ring] = nodes_t[...]
    for c in hy1:
        c.wait_recv()
    corners = []
    for d in range(2):
        x = CX - 1 if d == 0 else 0
        for side in range(2):
            for q in range(2):
                i = 2 * side + q
                cs[d, i : i + 1, :] = yr[0, side, q, x : x + 1, :]
        corners.append(
            pltpu.make_async_remote_copy(
                cs.at[d], cr.at[d], css.at[d], crs.at[d],
                device_id=gx_peer(1 if d == 0 else NGX - 1),
            )
        )
        corners[d].start()
    unpack_y(f0, 0, range(4))
    pl.semaphore_wait(known.at[0], 2 + len(ring_peers))
    tell(1, [z_peer(4), z_peer(nz - 4)])
    shapes_stage = spread(shapes_x, ring, x_peers, 2)
    lax.fori_loop(2, CX, first_layer, 0)
    for c in hx1:
        c.wait_recv()
    unpack_x(f0, 0, range(4))
    first_layer(1, 0)
    first_layer(CX, 0)


    for c in corners:
        c.wait_recv()
    for d in range(2):
        x, far, sign = (1, 0, 1.0) if d == 0 else (CX, CX + 1, -1.0)
        edge = gx == (0 if d == 0 else NGX - 1)
        for t in range(YT):
            rows, own = slice(Y0 + 8 * t, Y0 + 8 * t + 8), slice(8 * t, 8 * t + 8)
            u, p = f0[0, x, rows, :], f0[3, x, rows, :]
            nu = time_step * xr[0, d, 5, own, :].astype(f32)
            tile = xr[0, d, 4, own, :].astype(f32) + (nu * u + sign * (w_row * u - half * p))
            if t == 0:
                corner = jnp.where(gy == 0, 0.0, cr[d, 1:2, :])
                tile = tile + jnp.where(x8 == 0, nu * corner, 0.0)
            if t == YT - 1:
                corner = jnp.where(gy == NGY - 1, 0.0, cr[d, 3:4, :])
                tile = tile + jnp.where(x8 == 7, nu * corner, 0.0)
            f1[0, far, rows, :] = jnp.where(edge, 0.0, tile)
    for d in range(2):
        sign = 1.0 if d == 0 else -1.0
        edge = gy == (0 if d == 0 else NGY - 1)
        u, p = ys[0, 1 - d, 0], ys[0, 1 - d, 3]
        nu = time_step * yr[0, d, 5]
        low = jnp.where(gx == 0, 0.0, cr[0, 2 * d : 2 * d + 1, :])
        high = jnp.where(gx == NGX - 1, 0.0, cr[1, 2 * d : 2 * d + 1, :])
        tile = yr[0, d, 4] + (nu * u - (sign * half) * p)
        tile = tile + jnp.where(x8 == 0, (nu - w_row) * low, 0.0)
        tile = tile + jnp.where(x8 == CX - 1, (nu + w_row) * high, 0.0)
        yi[d, 0] = jnp.where(edge, 0.0, tile)
        y = Y0 - 1 if d == 0 else Y0 + CY
        for x in range(CX):
            f1[1, x + 1, y : y + 1, :] = yi[d, 0, x : x + 1, :]

    def second_pressure(x, carry):
        for t in range(YT):
            pre_o[x - 1, 8 * t : 8 * t + 8, :] = pressure_tile(f1, x, t)
        return carry

    lax.fori_loop(1, CX + 1, second_pressure, 0)

    for s in range(SL):
        line = cell_s[0, s] >> 8
        layer = line // CY
        samp[s : s + 1, :] = pre_o[layer, pl.ds(line - layer * CY, 1), :]
    sampled = jnp.sum(jnp.where(z_mask, samp[...], 0.0), axis=1, keepdims=True)
    load = (own_area * sampled).astype(bf16).astype(f32)
    g0[plane, 0:1, :] = row_of(load, SL * parity)
    ring_stage.wait_recv()
    g0[plane, 1:2, :] = jnp.sum(ring_b[:, 0:1, :], axis=0)
    pl.semaphore_wait(known.at[1], 2)
    stage0 = spread(g0, plane, z_peers, 3)
    for c in hx1 + hy1 + corners + [ring_stage, damper_stage]:
        c.wait_send()
    damper_stage.wait_recv()

    def table(i, carry):
        low = panels[pl.ds(2 * i + ring // 2, 1), :] & 127
        sub = lax.broadcasted_iota(jnp.int32, (128, 128), 0)
        onehot[:, pl.ds(pl.multiple_of(i * 128, 128), 128)] = (sub == low).astype(f32).astype(bf16)
        return carry

    lax.fori_loop(0, nz, table, 0)

    def paired(buf, row):
        return jnp.concatenate(
            [buf[2 * j, row : row + 1, :] + buf[2 * j + 1, row : row + 1, :] for j in range(NGY // 2)],
            axis=0,
        )

    visc_all, hyst_all, node_all = (paired(dampers_b, r) for r in range(3))
    for j in range(NGY // 2):
        pick_all[:, j * 128 : (j + 1) * 128] = pick(node_all[j : j + 1, :])
    q0_row, v0_row, omega, zeta = (jnp.sum(ring_b[:, r : r + 1, :], axis=0) for r in range(1, 5))

    shapes_stage.wait_recv()
    nodes_stage = spread(nodes_x, ring, x_peers, 4)
    stage0.wait_recv()
    sub16 = lax.broadcasted_iota(jnp.int32, (16, 128), 0)
    for i in range(nz):
        high = panels[pl.ds(2 * i + ring // 2, 1), :] >> 7
        lhs[:, i * 128 : (i + 1) * 128] = jnp.where(sub16 == high, g0[i, 0:1, :], 0.0).astype(bf16)
    placed = lax.dot_general(
        lhs[...], onehot[...], (((1,), (1,)), ((), ())), preferred_element_type=f32
    )
    parts = []
    for r in range(RX):
        part = jnp.zeros((MB, 128), f32)
        for a in range(16):
            part = part + shapes_x[r, :, a * 128 : (a + 1) * 128].astype(f32) * placed[a : a + 1, :]
        parts.append(row_of(jnp.sum(part, axis=1, keepdims=True), MB * r))

    def response(stretch, rate, viscous, hysteretic, hysteresis):
        hysteresis = hysteresis + modal_step * (
            hysteresis_gain * rate
            - shape_beta * jnp.abs(rate) * hysteresis
            - shape_gamma * rate * jnp.abs(hysteresis)
        )
        return hysteresis, -(viscous * rate + spring_rate * stretch + hysteretic * hysteresis)

    first = jnp.sum(g0[:, 1:2, :], axis=0)
    stretch0 = first[:, 0:DB]
    hysteresis, force = response(stretch0, first[:, DB : 2 * DB], dvisc[...], dhyst[...], dstate[...])
    damper_part = jnp.sum(drift[:, 0:DB] * force, axis=1, keepdims=True)
    spot = ring * NGY + gy
    h1[spot, 0:1, :] = (parts[0] + parts[1]) + (parts[2] + parts[3])
    h1[spot, 1:2, :] = row_of(damper_part, MB * ring)
    h1[spot, 2:3, :] = placed_half(stretch0)
    h1[spot, 3:4, :] = placed_half(hysteresis)

    plane_peers = []
    steps = [(a, b, c) for a in range(RX) for b in range(NGY // 2) for c in range(2)]
    for a, b, c in sorted(steps, key=lambda k: -min(k[0], RX - k[0]) - min(k[1], NGY // 2 - k[1])):
        if a or b or c:
            there = 2 * lax.rem(gy // 2 + b, NGY // 2) + lax.rem(odd + c, 2)
            plane_peers.append({"gx": plane * RX + lax.rem(ring + a, RX), "gy": there})
    stage1 = spread(h1, spot, plane_peers, 5)
    stage0.wait_send()
    shapes_stage.wait_send()
    nodes_stage.wait_recv()
    drift_x[...] = jnp.dot(
        nodes_x[...].reshape(RX * MB, -1), pick_all[...], preferred_element_type=f32
    )
    pack_x(f1, 1, (1, 2, 3))
    pack_y(f1, 1, (1, 2, 3))
    hx3 = [x_copy(1, 1, d, 1, 4) for d in range(2)]
    hy3 = [y_copy(1, 1, d, 1, 4) for d in range(2)]
    for c in hx3 + hy3:
        c.start()
    nodes_stage.wait_send()
    stage1.wait_recv()
    panel_modal = jnp.sum(h1[:, 0:1, :], axis=0)
    damper_modal = jnp.sum(h1[:, 1:2, :], axis=0)
    stretch_all, hysteresis_all = paired(h1, 2), paired(h1, 3)

    def advance_modes(q, v, damper_load):
        acceleration = (
            panel_modal + damper_load - 2.0 * zeta * omega * v - omega * omega * q
        )
        v = v + modal_step * acceleration
        return q + modal_step * v, v

    q1, v1 = advance_modes(q0_row, v0_row, damper_modal)
    v1_column = column_of(v1, RX * MB)
    for j in range(NGY // 2):
        g2[plane, j : j + 1, :] = jnp.sum(
            drift_x[:, j * 128 : (j + 1) * 128] * v1_column, axis=0, keepdims=True
        )
    stage2 = spread(g2, plane, z_peers, 6)
    stage1.wait_send()
    for c in hx3 + hy3:
        c.wait_recv()
    unpack_x(f1, 1, (1, 2, 3))
    unpack_y(f1, 1, (1, 2, 3))

    def second_velocity(x, carry):
        for t in range(YT):
            new = velocity_tile(f1, x, t)
            for k in range(3):
                vel_o[k, x - 1, 8 * t : 8 * t + 8, :] = new[k]
        return carry

    lax.fori_loop(1, CX + 1, second_velocity, 0)
    for c in hx3 + hy3:
        c.wait_send()
    stage2.wait_recv()
    rate_all = jnp.sum(g2[...], axis=0)
    stretch_all = stretch_all + modal_step * rate_all
    hysteresis_all, force = response(stretch_all, rate_all, visc_all, hyst_all, hysteresis_all)
    late[...] = hysteresis_all
    own = late[pl.ds(gy // 2, 1), :]
    damp_o[...] = jnp.where(odd == 1, own[:, DB : 2 * DB], own[:, 0:DB])
    part = jnp.zeros((MB, 128), f32)
    for j in range(NGY // 2):
        rows = pl.ds(pl.multiple_of(ring * MB, MB), MB)
        part = part + drift_x[rows, j * 128 : (j + 1) * 128] * force[j : j + 1, :]
    damper_modal = row_of(jnp.sum(part, axis=1, keepdims=True), MB * ring)
    q2, v2 = advance_modes(q1, v1, damper_modal)
    modal_o[0:1, :] = row_of(column_of(q2, MB, MB * ring), 0, MB)
    modal_o[1:2, :] = row_of(column_of(v2, MB, MB * ring), 0, MB)
    stage2.wait_send()


def write_out(*refs):
    n = len(refs) // 2
    sem = refs[-1]
    copies = [pltpu.make_async_copy(refs[i], refs[n + i], sem.at[i]) for i in range(n)]
    for c in copies:
        c.start()
    for c in copies:
        c.wait()


def body(
    velocity, pressure, viscosity, wind_profile, panel_area, slot_cell, slot_panel, panel_shapes,
    node_shapes, damper_node, damper_viscous, damper_hysteretic, frequency, damping_ratio,
    modal_state, damper_state,
):
    hbm = pl.BlockSpec(memory_space=pltpu.MemorySpace.HBM)
    vmem = pl.BlockSpec(memory_space=pltpu.VMEM)
    f32, bf16 = jnp.float32, jnp.bfloat16
    slots = slot_panel.shape[1]
    small = (
        wind_profile.reshape(1, -1), panel_area.reshape(1, -1),
        slot_cell, slot_cell, slot_panel.reshape(slots // 128, 128), panel_shapes.T, node_shapes.T,
        damper_node.reshape(1, -1), damper_viscous.reshape(1, -1), damper_hysteretic.reshape(1, -1),
        frequency.reshape(1, -1), damping_ratio.reshape(1, -1), modal_state,
        damper_state.reshape(1, -1),
    )
    outs = (
        jax.ShapeDtypeStruct(velocity.shape, f32),
        jax.ShapeDtypeStruct(pressure.shape, f32),
        jax.ShapeDtypeStruct(modal_state.shape, f32),
        jax.ShapeDtypeStruct((1, DB), f32),
    )
    held = [
        (pltpu.SMEM if i == 2 else pltpu.VMEM)(a.shape, a.dtype) for i, a in enumerate(small)
    ]
    results = pl.pallas_call(
        kernel,
        out_shape=outs,
        in_specs=[hbm] * (3 + len(small)),
        out_specs=(vmem,) * 4,
        scratch_shapes=held + [
            pltpu.VMEM((4, CX + 2, CY + 16, NZ), f32),
            pltpu.VMEM((4, CX + 2, CY + 16, NZ), f32),
            pltpu.VMEM((CX, CY, NZ), f32),
            pltpu.VMEM((2, 2, 6, CY, NZ), bf16),
            pltpu.VMEM((2, 2, 6, CY, NZ), bf16),
            pltpu.VMEM((2, 2, 6, CX, NZ), f32),
            pltpu.VMEM((2, 2, 6, CX, NZ), f32),
            pltpu.VMEM((2, 2, CX, NZ), f32),
            pltpu.VMEM((2, 4, NZ), f32),
            pltpu.VMEM((2, 4, NZ), f32),
            pltpu.VMEM((SL, NZ), f32),
            pltpu.VMEM((128, NGX // RX * 128), bf16),
            pltpu.VMEM((16, NGX // RX * 128), bf16),
            pltpu.VMEM((RX,) + panel_shapes.shape[::-1], bf16),
            pltpu.VMEM((RX,) + node_shapes.shape[::-1], bf16),
            pltpu.VMEM((node_shapes.shape[0], DB * NGY), bf16),
            pltpu.VMEM((RX * MB, DB * NGY), f32),
            pltpu.VMEM((RX, 8, 128), f32),
            pltpu.VMEM((NGY, 4, 128), f32),
            pltpu.VMEM((NGX // RX, 2, 128), f32),
            pltpu.VMEM((RX * NGY, 4, 128), f32),
            pltpu.VMEM((NGX // RX, NGY // 2, 128), f32),
            pltpu.VMEM((NGY // 2, 128), f32),
            pltpu.SemaphoreType.DMA((3,)),
            pltpu.SemaphoreType.DMA((len(small),)),
            pltpu.SemaphoreType.DMA((2, 4)),
            pltpu.SemaphoreType.DMA((2, 4)),
            pltpu.SemaphoreType.DMA((2, 4)),
            pltpu.SemaphoreType.DMA((2, 4)),
            pltpu.SemaphoreType.DMA((2,)),
            pltpu.SemaphoreType.DMA((2,)),
            pltpu.SemaphoreType.DMA((7,)),
            pltpu.SemaphoreType.DMA((7,)),
            pltpu.SemaphoreType.REGULAR((2,)),
        ],
        compiler_params=pltpu.CompilerParams(
            collective_id=0, has_side_effects=True, vmem_limit_bytes=40 << 20
        ),
    )(*[pltpu.with_memory_space_constraint(a, pltpu.MemorySpace.HBM) for a in (velocity, pressure, viscosity, *small)])
    vel, pre, modal, damp = pl.pallas_call(
        write_out,
        out_shape=outs,
        in_specs=[vmem] * 4,
        out_specs=(hbm,) * 4,
        scratch_shapes=[pltpu.SemaphoreType.DMA((4,))], compiler_params=pltpu.CompilerParams(vmem_limit_bytes=1 << 20),
    )(*results)
    return vel, pre, modal, damp.reshape(-1)


def solution(mesh):
    placed = (
        P(None, "gx", "gy", None),
        P("gx", "gy", None),
        P("gx", "gy", None),
        P(),
        P("gy"),
        P("gy", "gx"),
        P("gy", None),
        P("gy", "gx"),
        P(None, "gx"),
        P("gy"),
        P("gy"),
        P("gy"),
        P("gx"),
        P("gx"),
        P(None, "gx"),
        P("gy"),
    )
    return jax.shard_map(
        body,
        mesh=mesh,
        in_specs=placed,
        out_specs=(P(None, "gx", "gy", None), P("gx", "gy", None), P(None, "gx"), P("gy")),
        check_vma=False,
    )
```
